256 devices in a mesh: row: 16 (over x, y_hi, core), col: 16 (over z, y_lo).
Axes of the slice: x: 4, y: 4 (y_hi: 2, y_lo: 2; y = y_hi * 2 + y_lo), z: 8, core: 2. Of those that a mesh axis runs over, the one named last changes fastest.
Arguments:
- record: float32 [2, 262144], P(None, ('row', 'col')), may hold values from -5 to 5
Outputs:
- spectrum: float32 [256, 256, 16, 2, 256], P('row', 'col')
The draws below stay inside these ranges and needn't reach their ends.
All inputs are finite; a program needn't handle non-finite values.
Results may differ from the reference program's by a relative error of at most 0.00011.
Values sent between devices are 32-bit elements; how exact they have to be, the bound alone decides.
A program may use at most 64 MiB of HBM per device.

```python
import math
import jax
import jax.numpy as jnp
from jax import lax

C = 256
P_SIZE = 256
HOP = 64
FRAMES = 4096
SAMPLES = 262144


def block_scale(own_key, shape, shards, least, high):
    loudness = 1.0
    for dim, blocks in shards:
        draws = jax.random.uniform(jax.random.fold_in(jax.random.fold_in(own_key, 6), dim), (blocks,), jnp.float32, least / len(shards), high / len(shards))
        loudness = loudness * jnp.repeat(jnp.exp(draws), shape[dim] // blocks).reshape((-1,) + (1,) * (len(shape) - 1 - dim))
    return loudness


def scatter_about(stream_key, shape, spread, bound, pieces=(), held_as=jnp.bfloat16):
    level = block_scale(stream_key, shape, pieces, -0.22, 0.18) if pieces else 1.0
    values = jax.random.normal(stream_key, shape, jnp.float32) * spread * level
    return jnp.minimum(jnp.maximum(values, -bound), bound).astype(held_as)


def setup_inputs(seed: int = 0) -> dict:
    splits = jax.random.split(jax.random.key(seed), 2)
    return {
        "record": scatter_about(splits[0], (2, SAMPLES), 0.7, 5.0, ((1, 256),), jnp.float32),
    }


highest = lax.Precision.HIGHEST

def spectral_table(length, start_column, width, weights):
    position = jnp.arange(length, dtype=jnp.int32)
    column = start_column + jnp.arange(width, dtype=jnp.int32)
    turns = position[:, None] * column[None, :] % length
    phase = turns.astype(jnp.float32) * (2.0 * math.pi / length)
    cosine = weights[:, None] * jnp.cos(phase)
    sinus = weights[:, None] * jnp.sin(phase)
    upper = jnp.stack([cosine, -sinus], axis=1)
    bottom = jnp.stack([sinus, cosine], axis=1)
    return jnp.stack([upper, bottom], axis=0)

def hann_weights():
    position = jnp.arange(C, dtype=jnp.int32).astype(jnp.float32)
    return (0.5 - 0.5 * jnp.cos(position * (2.0 * math.pi / C))) / math.sqrt(3.0 * C / 8.0)

def framed(samples, amount):
    blocks = samples.reshape(2, amount + C // HOP - 1, HOP)
    return jnp.concatenate([blocks[:, offset:offset + amount] for offset in range(C // HOP)], axis=2)

def downconvert(spectra, start_channel, start_frame):
    channel = start_channel + jnp.arange(spectra.shape[1], dtype=jnp.int32)
    moment = start_frame + jnp.arange(spectra.shape[2], dtype=jnp.int32)
    turns = (channel * HOP % C)[:, None] * (moment % C)[None, :] % C
    phase = turns.astype(jnp.float32) * (2.0 * math.pi / C)
    cosine = jnp.cos(phase)
    sinus = jnp.sin(phase)
    real_part = spectra[0] * cosine + spectra[1] * sinus
    imag_part = spectra[1] * cosine - spectra[0] * sinus
    return jnp.stack([real_part, imag_part])

def channelize(frames, start_channel, width, start_frame):
    weights = spectral_table(C, start_channel, width, hann_weights())
    spectra = lax.dot_general(weights, frames, (((0, 1), (0, 2)), ((), ())), precision=highest, preferred_element_type=jnp.float32)
    return downconvert(spectra, start_channel, start_frame)

def correlate(leading, trailing):
    lead_count = leading.shape[1]
    trail_count = trailing.shape[1]
    windows = leading.shape[2] // P_SIZE
    lead = leading.reshape(2, lead_count, windows, P_SIZE)
    trail = trailing.reshape(2, trail_count, windows, P_SIZE)
    real_part = lead[0][:, None] * trail[0][None] + lead[1][:, None] * trail[1][None]
    imag_part = lead[1][:, None] * trail[0][None] - lead[0][:, None] * trail[1][None]
    weights = spectral_table(P_SIZE, 0, P_SIZE, jnp.full((P_SIZE,), 1.0 / math.sqrt(P_SIZE), jnp.float32))
    real_table = weights[0].reshape(P_SIZE, 2 * P_SIZE)
    imag_table = weights[1].reshape(P_SIZE, 2 * P_SIZE)
    dims = (((3,), (0,)), ((), ()))
    result = lax.dot_general(real_part, real_table, dims, precision=highest, preferred_element_type=jnp.float32)
    result = result + lax.dot_general(imag_part, imag_table, dims, precision=highest, preferred_element_type=jnp.float32)
    return result.reshape(lead_count, trail_count, windows, 2, P_SIZE)

def reference(record):
    samples = jnp.concatenate([record, jnp.zeros((2, C - HOP), jnp.float32)], axis=1)
    frames = framed(samples, FRAMES)
    spectra = channelize(frames, 0, C, 0)

    def one_channel(which):
        leading = lax.dynamic_slice_in_dim(spectra, which, 1, 1)
        return correlate(leading, spectra)[0]
    return lax.map(one_channel, jnp.arange(C, dtype=jnp.int32))
```

```python
import math

import jax
import jax.numpy as jnp
import numpy as np
from jax import lax
from jax.experimental import pallas as pl
from jax.experimental.pallas import tpu as pltpu
from jax.sharding import PartitionSpec as P

C = 256
P_SIZE = 256
HOP = 64
LANES = 128
WIDTH = 16
WINDOWS = 16
ROWS = 2048
PIECES = 3
DEPTH = PIECES * 2 * LANES


def channel_tables():
    position = np.arange(PIECES * LANES)
    table = np.zeros((PIECES, 2, LANES, 2, 2, WIDTH))
    turned = np.zeros_like(table)
    for parity in range(2):
        m = position - HOP * parity
        inside = (m >= 0) & (m < C)
        hann = np.where(inside, (0.5 - 0.5 * np.cos(2 * np.pi * m / C)) / math.sqrt(3 * C / 8), 0.0)
        turns = (position[:, None] * np.arange(WIDTH)[None]) % C
        w = hann[:, None] * np.exp(-2j * np.pi * turns / C)
        for part, v in enumerate((w, 1j * w)):
            v = v.reshape(PIECES, LANES, WIDTH)
            table[:, part, :, parity, 0] = v.real
            table[:, part, :, parity, 1] = v.imag
            turned[:, part, :, parity, 0] = v.imag
            turned[:, part, :, parity, 1] = -v.real
    tables = np.stack([table, turned]).reshape(2, DEPTH, 64)
    tables = np.concatenate([tables, tables], axis=2)
    angle = 2 * np.pi * (np.arange(16)[:, None] * np.arange(16)[None] % 16) / 16
    turns = np.stack([np.cos(angle), np.sin(angle)])
    turns = np.broadcast_to(turns[..., None], (2, 16, 16, LANES))
    return tables.astype(np.float32), np.ascontiguousarray(turns).astype(np.float32)


def second_tables():
    frame = np.arange(LANES)
    bins = np.arange(LANES)
    out = []
    for parity in range(2):
        turns = ((2 * frame[:, None] + parity) * bins[None]) % P_SIZE
        angle = 2 * np.pi * turns / P_SIZE
        c, s = np.cos(angle) / 16.0, np.sin(angle) / 16.0
        out.append(np.concatenate([np.concatenate([c, -s], 1), np.concatenate([s, c], 1)], 0))
    full = np.stack(out).astype(np.float32)
    high = full.astype(jnp.bfloat16)
    low = (full - high.astype(np.float32)).astype(jnp.bfloat16)
    return np.stack([high, low])


def signs():
    channel = np.arange(LANES) % WIDTH
    frame = np.arange(LANES)
    return np.where((channel[:, None] * frame[None]) % 2 == 1, -1.0, 1.0).astype(np.float32)


def halves(value):
    high = value.astype(jnp.bfloat16)
    low = (value - high.astype(jnp.float32)).astype(jnp.bfloat16)
    return high, low


def dot(a, b):
    return lax.dot_general(a, b, (((1,), (0,)), ((), ())), preferred_element_type=jnp.float32)


def channelize(gathered, tables, turns, sign, base):
    row = lax.axis_index("row")
    col = lax.axis_index("col")
    lane = lax.broadcasted_iota(jnp.int32, (16, LANES), 1)
    cosine = jnp.where(lane < 64, turns[0, row], turns[0, col])
    sinus = jnp.where(lane < 64, turns[1, row], turns[1, col])
    groups = DEPTH // 16
    shaped = tables[...].reshape(2, groups, 16, LANES)
    weights = (shaped[0] * cosine[None] + shaped[1] * sinus[None]).reshape(DEPTH, LANES)
    high_w, low_w = halves(weights)
    both = jnp.concatenate([high_w, low_w], axis=1)
    step = 512

    def block(i, _):
        start = pl.multiple_of(i * (2 * step), 2 * step)
        pieces = [gathered[pl.ds(start + j, step, stride=2), :] for j in range(2 * PIECES)]
        high, low = halves(jnp.concatenate(pieces, axis=1))
        wide = dot(high, both)
        result = wide[:, :LANES] + wide[:, LANES:] + dot(low, high_w)
        for k in range(step // LANES):
            turned = result[k * LANES : (k + 1) * LANES].T * sign[...]
            base[pl.ds(i * (step // LANES) + k, LANES, stride=WINDOWS), :] = turned
        return 0

    lax.fori_loop(0, ROWS // step, block, 0)


def correlate(a, base, second, out):
    def tile(first, count):
        return base[pl.ds(pl.multiple_of(first * WINDOWS, WINDOWS), count * WINDOWS), :]

    sums = []
    for parity in range(2):
        lead_re = tile(parity * 32 + a, 1)[None]
        lead_im = tile(parity * 32 + 16 + a, 1)[None]
        trail_re = tile(64 + parity * 32, 16).reshape(WIDTH, WINDOWS, LANES)
        trail_im = tile(64 + parity * 32 + 16, 16).reshape(WIDTH, WINDOWS, LANES)
        real = (lead_re * trail_re + lead_im * trail_im).reshape(256, LANES)
        imag = (lead_im * trail_re - lead_re * trail_im).reshape(256, LANES)
        high, low = halves(jnp.concatenate([real, imag], axis=1))
        sums.append(dot(high, second[0, parity]) + dot(low, second[0, parity]) + dot(high, second[1, parity]))
    total = sums[0] + sums[1]
    rest = sums[0] - sums[1]
    for j, value in enumerate((total[:, :LANES], total[:, LANES:], rest[:, :LANES], rest[:, LANES:])):
        out[pl.ds(j, 256, stride=4), :] = value


def kernel(gathered, tables, turns, sign, second, out, padded, base):
    a = pl.program_id(0)

    @pl.when(a == 0)
    def _():
        padded[0 : 2 * ROWS, :] = gathered[...]
        padded[2 * ROWS :, :] = jnp.zeros((8, LANES), jnp.float32)
        channelize(padded, tables, turns, sign, base)

    correlate(a, base, second, out)


def spectra(gathered):
    tables, turns = channel_tables()

    def whole(shape):
        return pl.BlockSpec(shape, lambda a: (0,) * len(shape), pipeline_mode=pl.Buffered(1))

    return pl.pallas_call(
        kernel,
        grid=(WIDTH,),
        out_shape=jax.ShapeDtypeStruct((WIDTH * 1024, LANES), jnp.float32),
        in_specs=[
            whole((2 * ROWS, LANES)),
            whole((2, DEPTH, LANES)),
            whole((2, 16, 16, LANES)),
            whole((LANES, LANES)),
            whole((2, 2, 256, 256)),
        ],
        out_specs=pl.BlockSpec((1024, LANES), lambda a: (a, 0)),
        scratch_shapes=[
            pltpu.VMEM((2 * ROWS + 8, LANES), jnp.float32),
            pltpu.VMEM((LANES * WINDOWS, LANES), jnp.float32),
        ],
        compiler_params=pltpu.CompilerParams(dimension_semantics=("arbitrary",)),
    )(gathered, jnp.asarray(tables), jnp.asarray(turns), jnp.asarray(signs()), jnp.asarray(second_tables()))


def local(record):
    tiles = record.reshape(2, 8, LANES).transpose(1, 0, 2).reshape(16, LANES)
    gathered = lax.all_gather(tiles, ("row", "col"), axis=0, tiled=True)
    result = spectra(gathered)
    result = result.reshape(WIDTH, WIDTH, WINDOWS, 2, 2, LANES)
    result = result.transpose(0, 1, 2, 4, 3, 5)
    return result.reshape(WIDTH, WIDTH, WINDOWS, 2, 2 * LANES)


def solution(mesh):
    return jax.shard_map(
        local,
        mesh=mesh,
        in_specs=(P(None, ("row", "col")),),
        out_specs=P("row", "col", None, None, None),
        check_vma=False,
    )
```

```python
import math

import jax
import jax.numpy as jnp
import numpy as np
from jax import lax
from jax.experimental import pallas as pl
from jax.experimental.pallas import tpu as pltpu
from jax.sharding import PartitionSpec as P

C = 256
P_SIZE = 256
HOP = 64
LANES = 128
WIDTH = 16
WINDOWS = 16
ROWS = 2048
PIECES = 3
DEPTH = PIECES * 2 * LANES


def channel_tables():
    position = np.arange(PIECES * LANES)
    table = np.zeros((PIECES, 2, LANES, 2, 2, WIDTH))
    turned = np.zeros_like(table)
    for parity in range(2):
        m = position - HOP * parity
        inside = (m >= 0) & (m < C)
        hann = np.where(inside, (0.5 - 0.5 * np.cos(2 * np.pi * m / C)) / math.sqrt(3 * C / 8), 0.0)
        turns = (position[:, None] * np.arange(WIDTH)[None]) % C
        w = hann[:, None] * np.exp(-2j * np.pi * turns / C)
        for part, v in enumerate((w, 1j * w)):
            v = v.reshape(PIECES, LANES, WIDTH)
            table[:, part, :, parity, 0] = v.real
            table[:, part, :, parity, 1] = v.imag
            turned[:, part, :, parity, 0] = v.imag
            turned[:, part, :, parity, 1] = -v.real
    tables = np.stack([table, turned]).reshape(2, DEPTH, 64)
    tables = np.concatenate([tables, tables], axis=2)
    angle = 2 * np.pi * (np.arange(16)[:, None] * np.arange(16)[None] % 16) / 16
    turns = np.stack([np.cos(angle), np.sin(angle)])
    turns = np.broadcast_to(turns[..., None], (2, 16, 16, LANES))
    return tables.astype(np.float32), np.ascontiguousarray(turns).astype(np.float32)


def second_tables():
    frame = np.arange(LANES)
    bins = np.arange(LANES)
    out = []
    for parity in range(2):
        turns = ((2 * frame[:, None] + parity) * bins[None]) % P_SIZE
        angle = 2 * np.pi * turns / P_SIZE
        c, s = np.cos(angle) / 16.0, np.sin(angle) / 16.0
        out.append(np.concatenate([np.concatenate([c, -s], 1), np.concatenate([s, c], 1)], 0))
    full = np.stack(out).astype(np.float32)
    high = full.astype(jnp.bfloat16)
    low = (full - high.astype(np.float32)).astype(jnp.bfloat16)
    return np.stack([high, low])


def signs():
    channel = np.arange(LANES) % WIDTH
    frame = np.arange(LANES)
    return np.where((channel[:, None] * frame[None]) % 2 == 1, -1.0, 1.0).astype(np.float32)


def halves(value):
    high = value.astype(jnp.bfloat16)
    low = (value - high.astype(jnp.float32)).astype(jnp.bfloat16)
    return high, low


def dot(a, b):
    return lax.dot_general(a, b, (((1,), (0,)), ((), ())), preferred_element_type=jnp.float32)


def channelize(gathered, tables, turns, sign, base):
    row = lax.axis_index("row")
    col = lax.axis_index("col")
    lane = lax.broadcasted_iota(jnp.int32, (16, LANES), 1)
    cosine = jnp.where(lane < 64, turns[0, row], turns[0, col])
    sinus = jnp.where(lane < 64, turns[1, row], turns[1, col])
    groups = DEPTH // 16
    shaped = tables[...].reshape(2, groups, 16, LANES)
    weights = (shaped[0] * cosine[None] + shaped[1] * sinus[None]).reshape(DEPTH, LANES)
    high_w, low_w = halves(weights)
    both = jnp.concatenate([high_w, low_w], axis=1)
    step = 512

    def block(i, _):
        start = pl.multiple_of(i * (2 * step), 2 * step)
        pieces = [gathered[pl.ds(start + j, step, stride=2), :] for j in range(2 * PIECES)]
        high, low = halves(jnp.concatenate(pieces, axis=1))
        wide = dot(high, both)
        result = wide[:, :LANES] + wide[:, LANES:] + dot(low, high_w)
        for k in range(step // LANES):
            turned = result[k * LANES : (k + 1) * LANES].T * sign[...]
            base[pl.ds(i * (step // LANES) + k, LANES, stride=WINDOWS), :] = turned
        return 0

    lax.fori_loop(0, ROWS // step, block, 0)


def correlate(a, base, second, out):
    def tile(first, count):
        return base[pl.ds(pl.multiple_of(first * WINDOWS, WINDOWS), count * WINDOWS), :]

    sums = []
    for parity in range(2):
        lead_re = tile(parity * 32 + a, 1)[None]
        lead_im = tile(parity * 32 + 16 + a, 1)[None]
        trail_re = tile(64 + parity * 32, 16).reshape(WIDTH, WINDOWS, LANES)
        trail_im = tile(64 + parity * 32 + 16, 16).reshape(WIDTH, WINDOWS, LANES)
        real = (lead_re * trail_re + lead_im * trail_im).reshape(256, LANES)
        imag = (lead_im * trail_re - lead_re * trail_im).reshape(256, LANES)
        high, low = halves(jnp.concatenate([real, imag], axis=1))
        sums.append(dot(high, second[0, parity]) + dot(low, second[0, parity]) + dot(high, second[1, parity]))
    total = sums[0] + sums[1]
    rest = sums[0] - sums[1]
    for j, value in enumerate((total[:, :LANES], total[:, LANES:], rest[:, :LANES], rest[:, LANES:])):
        out[pl.ds(j, 256, stride=4), :] = value


def kernel(gathered, tables, turns, sign, second, out, padded, base):
    a = pl.program_id(0)

    @pl.when(a == 0)
    def _():
        padded[0 : 2 * ROWS, :] = gathered[...]
        padded[2 * ROWS :, :] = jnp.zeros((8, LANES), jnp.float32)
        channelize(padded, tables, turns, sign, base)

    correlate(a, base, second, out)


def spectra(gathered):
    tables, turns = channel_tables()

    def whole(shape):
        return pl.BlockSpec(shape, lambda a: (0,) * len(shape), pipeline_mode=pl.Buffered(1))

    return pl.pallas_call(
        kernel,
        grid=(WIDTH,),
        out_shape=jax.ShapeDtypeStruct((WIDTH * 1024, LANES), jnp.float32),
        in_specs=[
            whole((2 * ROWS, LANES)),
            whole((2, DEPTH, LANES)),
            whole((2, 16, 16, LANES)),
            whole((LANES, LANES)),
            whole((2, 2, 256, 256)),
        ],
        out_specs=pl.BlockSpec((1024, LANES), lambda a: (a, 0)),
        scratch_shapes=[
            pltpu.VMEM((2 * ROWS + 8, LANES), jnp.float32),
            pltpu.VMEM((LANES * WINDOWS, LANES), jnp.float32),
        ],
        compiler_params=pltpu.CompilerParams(dimension_semantics=("arbitrary",)),
    )(gathered, jnp.asarray(tables), jnp.asarray(turns), jnp.asarray(signs()), jnp.asarray(second_tables()))


MESH = pl.DeviceIdType.MESH
PLUS = (0, 1)


def gather_kernel(own, out, copied, z_send, z_recv, far_send, far_recv, near_send, near_recv, core_send, core_recv):
    row = lax.axis_index("row")
    col = lax.axis_index("col")
    core = lax.rem(row, 2)
    x = lax.div(row, 4)
    y = lax.rem(lax.div(row, 2), 2) * 2 + lax.rem(col, 2)
    z = lax.div(col, 2)

    def device(x, y, z, core):
        return (x * 4 + lax.div(y, 2) * 2 + core, z * 2 + lax.rem(y, 2))

    def moved(value, distance, length=4):
        return lax.rem(value + (distance + length), length)

    def piece(half, x, y):
        return out.at[x, lax.div(y, 2), core, pl.ds(4 * half, 4), lax.rem(y, 2)]

    started = []

    def send(source, target, send_sem, recv_sem, to):
        copy = pltpu.make_async_remote_copy(
            src_ref=source, dst_ref=target, send_sem=send_sem, recv_sem=recv_sem, device_id=to, device_id_type=MESH
        )
        copy.start()
        started.append(copy)

    def arrived(ref, recv_sem):
        pltpu.make_async_copy(ref, ref, recv_sem).wait()

    barrier = pltpu.get_barrier_semaphore()
    peers = [device(x, y, moved(z, d, 8), core) for d in range(1, 8)]
    peers += [device(moved(x, d), y, z, core) for d in range(1, 4)]
    peers += [device(x, moved(y, d), z, core) for d in range(1, 4)]
    peers += [device(x, y, z, 1 - core)]
    for peer in peers:
        pl.semaphore_signal(barrier, inc=1, device_id=peer, device_id_type=MESH)
    here = out.at[x, lax.div(y, 2), core, z, lax.rem(y, 2)]
    local_copy = pltpu.make_async_copy(own, here, copied)
    local_copy.start()
    pl.semaphore_wait(barrier, len(peers))

    for d in (4, 3, 5, 2, 6, 1, 7):
        send(own, here, z_send.at[d - 1], z_recv.at[d - 1], device(x, y, moved(z, d, 8), core))
    local_copy.wait()
    for d in (1, 7, 2, 6, 3, 5, 4):
        arrived(out.at[x, lax.div(y, 2), core, moved(z, -d, 8), lax.rem(y, 2)], z_recv.at[d - 1])

    def along(half, distance_first, distance_second):
        if half == 0:
            return moved(x, distance_first), moved(y, distance_second)
        return moved(x, distance_second), moved(y, distance_first)

    def to_core(half, j, k):
        ref = piece(half, *along(half, j, k))
        index = half * 16 + j * 4 + k
        send(ref, ref, core_send.at[index], core_recv.at[index], device(x, y, z, 1 - core))

    def to_second(half, j, k, e, slot):
        ref = piece(half, *along(half, j, k))
        index = half * 12 + slot * 4 + j
        px, py = along(half, 0, e)
        send(ref, ref, near_send.at[index], near_recv.at[index], device(px, py, z, core))

    def first_arrived(half, d):
        j = (4 - d) % 4
        arrived(piece(half, *along(half, j, 0)), far_recv.at[half * 3 + d - 1])
        to_second(half, j, 0, 1, 0)
        to_second(half, j, 0, -1, 1)
        to_core(half, j, 0)

    def second_arrived(half, j, slot):
        k = (3, 1, 2)[slot]
        arrived(piece(half, *along(half, j, k)), near_recv.at[half * 12 + slot * 4 + j])
        if slot == 0 and j in PLUS:
            to_second(half, j, k, 1, 2)
        if slot == 1 and j not in PLUS:
            to_second(half, j, k, -1, 2)
        to_core(half, j, k)

    for half in range(2):
        ref = piece(half, x, y)
        for d in (1, 3, 2):
            px, py = along(half, d, 0)
            index = half * 3 + d - 1
            send(ref, ref, far_send.at[index], far_recv.at[index], device(px, py, z, core))
        to_second(half, 0, 0, 1, 0)
        to_second(half, 0, 0, -1, 1)
    for half in range(2):
        to_core(half, 0, 0)
    for d in (1, 3):
        for half in range(2):
            first_arrived(half, d)
    for slot in (0, 1):
        for half in range(2):
            second_arrived(half, 0, slot)
    for half in range(2):
        first_arrived(half, 2)
    for j in (3, 1, 2):
        for slot in (0, 1):
            for half in range(2):
                second_arrived(half, j, slot)
    for j in (0, 3, 1, 2):
        for half in range(2):
            second_arrived(half, j, 2)
    for half in range(2):
        for j in range(4):
            for k in range(4):
                px, py = along(half, j, k)
                ref = out.at[px, lax.div(py, 2), 1 - core, pl.ds(4 * half, 4), lax.rem(py, 2)]
                arrived(ref, core_recv.at[half * 16 + j * 4 + k])
    for copy in started:
        copy.wait_send()


def gather(tiles):
    def sems(count):
        return pltpu.SemaphoreType.DMA((count,))

    return pl.pallas_call(
        gather_kernel,
        out_shape=jax.ShapeDtypeStruct((4, 2, 2, 8, 2, 16, LANES), jnp.float32),
        in_specs=[pl.BlockSpec(memory_space=pltpu.VMEM)],
        out_specs=pl.BlockSpec(memory_space=pltpu.VMEM),
        scratch_shapes=[
            pltpu.SemaphoreType.DMA,
            sems(7), sems(7), sems(6), sems(6), sems(24), sems(24), sems(32), sems(32),
        ],
        compiler_params=pltpu.CompilerParams(collective_id=0, has_side_effects=True),
    )(tiles)


def local(record):
    tiles = record.reshape(2, 8, LANES).transpose(1, 0, 2).reshape(16, LANES)
    gathered = gather(tiles).reshape(2 * ROWS, LANES)
    result = spectra(gathered)
    result = result.reshape(WIDTH, WIDTH, WINDOWS, 2, 2, LANES)
    result = result.transpose(0, 1, 2, 4, 3, 5)
    return result.reshape(WIDTH, WIDTH, WINDOWS, 2, 2 * LANES)


def solution(mesh):
    return jax.shard_map(
        local,
        mesh=mesh,
        in_specs=(P(None, ("row", "col")),),
        out_specs=P("row", "col", None, None, None),
        check_vma=False,
    )
```

```python
import math

import jax
import jax.numpy as jnp
import numpy as np
from jax import lax
from jax.experimental import pallas as pl
from jax.experimental.pallas import tpu as pltpu
from jax.sharding import PartitionSpec as P

C = 256
P_SIZE = 256
HOP = 64
LANES = 128
WIDTH = 16
WINDOWS = 16
ROWS = 2048
PIECES = 3
DEPTH = PIECES * 2 * LANES
MESH = pl.DeviceIdType.MESH
ORDER = (0, 1, 7, 2, 6, 3, 5, 4)
SLOTS = 4


def channel_tables():
    position = np.arange(PIECES * LANES)
    table = np.zeros((PIECES, 2, LANES, 2, 2, WIDTH))
    turned = np.zeros_like(table)
    for parity in range(2):
        m = position - HOP * parity
        inside = (m >= 0) & (m < C)
        hann = np.where(inside, (0.5 - 0.5 * np.cos(2 * np.pi * m / C)) / math.sqrt(3 * C / 8), 0.0)
        turns = (position[:, None] * np.arange(WIDTH)[None]) % C
        w = hann[:, None] * np.exp(-2j * np.pi * turns / C)
        for part, v in enumerate((w, 1j * w)):
            v = v.reshape(PIECES, LANES, WIDTH)
            table[:, part, :, parity, 0] = v.real
            table[:, part, :, parity, 1] = v.imag
            turned[:, part, :, parity, 0] = v.imag
            turned[:, part, :, parity, 1] = -v.real
    tables = np.stack([table, turned]).reshape(2, DEPTH, 64)
    tables = np.concatenate([tables, tables], axis=2)
    angle = 2 * np.pi * (np.arange(16)[:, None] * np.arange(16)[None] % 16) / 16
    turns = np.stack([np.cos(angle), np.sin(angle)])
    turns = np.broadcast_to(turns[..., None], (2, 16, 16, LANES))
    return tables.astype(np.float32), np.ascontiguousarray(turns).astype(np.float32)


def second_tables():
    frame = np.arange(LANES)
    bins = np.arange(LANES)
    out = []
    for parity in range(2):
        turns = ((2 * frame[:, None] + parity) * bins[None]) % P_SIZE
        angle = 2 * np.pi * turns / P_SIZE
        c, s = np.cos(angle) / 16.0, np.sin(angle) / 16.0
        out.append(np.concatenate([np.concatenate([c, -s], 1), np.concatenate([s, c], 1)], 0))
    full = np.stack(out).astype(np.float32)
    high = full.astype(jnp.bfloat16)
    low = (full - high.astype(np.float32)).astype(jnp.bfloat16)
    return np.stack([high, low])


def signs():
    channel = np.arange(LANES) % WIDTH
    frame = np.arange(LANES)
    return np.where((channel[:, None] * frame[None]) % 2 == 1, -1.0, 1.0).astype(np.float32)


def halves(value):
    high = value.astype(jnp.bfloat16)
    low = (value - high.astype(jnp.float32)).astype(jnp.bfloat16)
    return high, low


def dot(a, b):
    return lax.dot_general(a, b, (((1,), (0,)), ((), ())), preferred_element_type=jnp.float32)


def first_weights(tables, turns, weights):
    row = lax.axis_index("row")
    col = lax.axis_index("col")
    lane = lax.broadcasted_iota(jnp.int32, (16, LANES), 1)
    cosine = jnp.where(lane < 64, turns[0, row], turns[0, col])
    sinus = jnp.where(lane < 64, turns[1, row], turns[1, col])
    groups = DEPTH // 16
    shaped = tables[...].reshape(2, groups, 16, LANES)
    full = (shaped[0] * cosine[None] + shaped[1] * sinus[None]).reshape(DEPTH, LANES)
    high, low = halves(full)
    weights[:, :LANES] = high
    weights[:, LANES:] = low


def in_order(held, ordered):
    z = lax.div(lax.axis_index("col"), 2)

    def window(w, _):
        for o, d in enumerate(ORDER):
            place = lax.rem(z + d, 8) * 32
            for low in range(2):
                block = held[lax.div(w, 4), lax.rem(lax.div(w, 2), 2) * 2 + low, lax.rem(w, 2), o]
                ordered[pl.ds(pl.multiple_of(w * 256 + place + 16 * low, 16), 16), :] = block
        return 0

    lax.fori_loop(0, WINDOWS, window, 0)
    ordered[2 * ROWS :, :] = jnp.zeros((8, LANES), jnp.float32)


def channelize(ordered, weights, sign, base):
    step = 512

    def block(i, _):
        start = pl.multiple_of(i * (2 * step), 2 * step)
        pieces = [ordered[pl.ds(start + j, step, stride=2), :] for j in range(2 * PIECES)]
        high, low = halves(jnp.concatenate(pieces, axis=1))
        wide = dot(high, weights[...])
        result = wide[:, :LANES] + wide[:, LANES:] + dot(low, weights[:, :LANES])
        for k in range(step // LANES):
            turned = result[k * LANES : (k + 1) * LANES].T * sign[...]
            base[pl.ds(i * (step // LANES) + k, LANES, stride=WINDOWS), :] = turned
        return 0

    lax.fori_loop(0, ROWS // step, block, 0)


def correlate(a, base, second, out):
    def tile(first, count):
        return base[pl.ds(pl.multiple_of(first * WINDOWS, WINDOWS), count * WINDOWS), :]

    sums = []
    for parity in range(2):
        lead_re = tile(parity * 32 + a, 1)[None]
        lead_im = tile(parity * 32 + 16 + a, 1)[None]
        trail_re = tile(64 + parity * 32, 16).reshape(WIDTH, WINDOWS, LANES)
        trail_im = tile(64 + parity * 32 + 16, 16).reshape(WIDTH, WINDOWS, LANES)
        real = (lead_re * trail_re + lead_im * trail_im).reshape(256, LANES)
        imag = (lead_im * trail_re - lead_re * trail_im).reshape(256, LANES)
        high, low = halves(jnp.concatenate([real, imag], axis=1))
        sums.append(dot(high, second[0, parity]) + dot(low, second[0, parity]) + dot(high, second[1, parity]))
    total = sums[0] + sums[1]
    rest = sums[0] - sums[1]
    for j, value in enumerate((total[:, :LANES], total[:, LANES:], rest[:, :LANES], rest[:, LANES:])):
        out[pl.ds(j, 256, stride=4), :] = value


def kernel(base, second, out, buffer, sems):
    def store(a, slot):
        place = pl.ds(pl.multiple_of(a * 1024, 1024), 1024)
        return pltpu.make_async_copy(buffer.at[slot], out.at[place], sems.at[slot])

    def step(a, _):
        slot = lax.rem(a, SLOTS)

        @pl.when(a >= SLOTS)
        def _():
            store(a, slot).wait()

        correlate(a, base, second, buffer.at[slot])
        store(a, slot).start()
        return 0

    lax.fori_loop(0, WIDTH, step, 0)
    for a in range(WIDTH - SLOTS, WIDTH):
        store(a, a % SLOTS).wait()


def spectra(base):
    whole = pl.BlockSpec(memory_space=pltpu.VMEM)
    return pl.pallas_call(
        kernel,
        out_shape=jax.ShapeDtypeStruct((WIDTH * 1024, LANES), jnp.float32),
        in_specs=[whole, whole],
        out_specs=pl.BlockSpec(memory_space=pl.ANY),
        scratch_shapes=[pltpu.VMEM((SLOTS, 1024, LANES), jnp.float32), pltpu.SemaphoreType.DMA((SLOTS,))],
    )(base, jnp.asarray(second_tables()))


def gather_kernel(
    own, tables_hbm, turns_hbm, sign_hbm, base, out, ordered, tables, turns, sign, weights,
    loaded, copied, z_send, z_recv, far_send, far_recv, near_send, near_recv, core_send, core_recv
):
    row = lax.axis_index("row")
    col = lax.axis_index("col")
    core = lax.rem(row, 2)
    x = lax.div(row, 4)
    y = lax.rem(lax.div(row, 2), 2) * 2 + lax.rem(col, 2)
    z = lax.div(col, 2)

    def device(x, y, z, core):
        return (x * 4 + lax.div(y, 2) * 2 + core, z * 2 + lax.rem(y, 2))

    def moved(value, distance, length=4):
        return lax.rem(value + (distance + length), length)

    def piece(half, x, y):
        return out.at[x, y, core, pl.ds(4 * half, 4)]

    started = []

    def send(source, target, send_sem, recv_sem, to):
        copy = pltpu.make_async_remote_copy(
            src_ref=source, dst_ref=target, send_sem=send_sem, recv_sem=recv_sem, device_id=to, device_id_type=MESH
        )
        copy.start()
        started.append(copy)

    def arrived(ref, recv_sem):
        pltpu.make_async_copy(ref, ref, recv_sem).wait()

    barrier = pltpu.get_barrier_semaphore()
    peers = [device(x, y, moved(z, d, 8), core) for d in range(1, 8)]
    peers += [device(moved(x, d), y, z, core) for d in range(1, 4)]
    peers += [device(x, moved(y, d), z, core) for d in range(1, 4)]
    peers += [device(x, y, z, 1 - core)]
    for peer in peers:
        pl.semaphore_signal(barrier, inc=1, device_id=peer, device_id_type=MESH)
    here = out.at[x, y, core, 0]
    local_copy = pltpu.make_async_copy(own, here, copied)
    local_copy.start()
    loads = [
        pltpu.make_async_copy(source, target, loaded.at[i])
        for i, (source, target) in enumerate(((tables_hbm, tables), (turns_hbm, turns), (sign_hbm, sign)))
    ]
    for load in loads:
        load.start()
    pl.semaphore_wait(barrier, len(peers))

    for o in range(1, 8):
        target = out.at[x, y, core, o]
        send(own, target, z_send.at[o - 1], z_recv.at[o - 1], device(x, y, moved(z, -ORDER[o], 8), core))
    for load in loads:
        load.wait()
    first_weights(tables, turns, weights)
    local_copy.wait()

    def along(half, distance_first, distance_second):
        if half == 0:
            return moved(x, distance_first), moved(y, distance_second)
        return moved(x, distance_second), moved(y, distance_first)

    def to_core(half, j, k):
        ref = piece(half, *along(half, j, k))
        index = half * 16 + j * 4 + k
        send(ref, ref, core_send.at[index], core_recv.at[index], device(x, y, z, 1 - core))

    def to_second(half, j, k, e, slot):
        ref = piece(half, *along(half, j, k))
        index = half * 12 + slot * 4 + j
        px, py = along(half, 0, e)
        send(ref, ref, near_send.at[index], near_recv.at[index], device(px, py, z, core))

    def first_arrived(half, d):
        j = (4 - d) % 4
        arrived(piece(half, *along(half, j, 0)), far_recv.at[half * 3 + d - 1])
        second_sent(half, j)

    def second_arrived(half, j, slot):
        k = (3, 1, 2)[slot]
        arrived(piece(half, *along(half, j, k)), near_recv.at[half * 12 + slot * 4 + j])
        to_core(half, j, k)

    def z_arrived(half):
        for o in range(max(1, 4 * half), 4 * half + 4):
            arrived(out.at[x, y, core, o], z_recv.at[o - 1])

    def first_sent(half):
        ref = piece(half, x, y)
        for d in (1, 3, 2):
            px, py = along(half, d, 0)
            index = half * 3 + d - 1
            send(ref, ref, far_send.at[index], far_recv.at[index], device(px, py, z, core))
        second_sent(half, 0)

    def second_sent(half, j):
        to_second(half, j, 0, 1, 0)
        to_second(half, j, 0, -1, 1)
        to_second(half, j, 0, 2, 2)
        to_core(half, j, 0)

    z_arrived(0)
    first_sent(0)
    z_arrived(1)
    first_sent(1)
    for half in range(2):
        for d in (1, 3):
            first_arrived(half, d)
        for slot in (0, 1):
            second_arrived(half, 0, slot)
    for half in range(2):
        first_arrived(half, 2)
        for slot in (0, 1):
            for j in (3, 1):
                second_arrived(half, j, slot)
    for half in range(2):
        second_arrived(half, 0, 2)
        for slot in (0, 1):
            second_arrived(half, 2, slot)
    for half in range(2):
        for j in (3, 1, 2):
            second_arrived(half, j, 2)
    for half in range(2):
        for j in range(4):
            for k in range(4):
                px, py = along(half, j, k)
                arrived(out.at[px, py, 1 - core, pl.ds(4 * half, 4)], core_recv.at[half * 16 + j * 4 + k])
    in_order(out, ordered)
    channelize(ordered, weights, sign, base)
    for copy in started:
        copy.wait_send()


def gather(tiles):
    def sems(count):
        return pltpu.SemaphoreType.DMA((count,))

    tables, turns = channel_tables()
    anywhere = pl.BlockSpec(memory_space=pl.ANY)
    return pl.pallas_call(
        gather_kernel,
        out_shape=jax.ShapeDtypeStruct((LANES * WINDOWS, LANES), jnp.float32),
        in_specs=[pl.BlockSpec(memory_space=pltpu.VMEM), anywhere, anywhere, anywhere],
        out_specs=pl.BlockSpec(memory_space=pltpu.VMEM),
        scratch_shapes=[
            pltpu.VMEM((4, 4, 2, 8, 16, LANES), jnp.float32),
            pltpu.VMEM((2 * ROWS + 8, LANES), jnp.float32),
            pltpu.VMEM(tables.shape, jnp.float32),
            pltpu.VMEM(turns.shape, jnp.float32),
            pltpu.VMEM((LANES, LANES), jnp.float32),
            pltpu.VMEM((DEPTH, 2 * LANES), jnp.bfloat16),
            sems(3),
            pltpu.SemaphoreType.DMA,
            sems(7), sems(7), sems(6), sems(6), sems(24), sems(24), sems(32), sems(32),
        ],
        compiler_params=pltpu.CompilerParams(collective_id=0, has_side_effects=True),
    )(tiles, jnp.asarray(tables), jnp.asarray(turns), jnp.asarray(signs()))


def local(record):
    tiles = record.reshape(2, 8, LANES).transpose(1, 0, 2).reshape(16, LANES)
    result = spectra(gather(tiles))
    result = result.reshape(WIDTH, WIDTH, WINDOWS, 2, 2, LANES)
    result = result.transpose(0, 1, 2, 4, 3, 5)
    return result.reshape(WIDTH, WIDTH, WINDOWS, 2, 2 * LANES)


def solution(mesh):
    return jax.shard_map(
        local,
        mesh=mesh,
        in_specs=(P(None, ("row", "col")),),
        out_specs=P("row", "col", None, None, None),
        check_vma=False,
    )
```

```python
import math

import jax
import jax.numpy as jnp
import numpy as np
from jax import lax
from jax.experimental import pallas as pl
from jax.experimental.pallas import tpu as pltpu
from jax.sharding import PartitionSpec as P

C = 256
P_SIZE = 256
HOP = 64
LANES = 128
WIDTH = 16
WINDOWS = 16
ROWS = 2048
PIECES = 3
DEPTH = PIECES * 2 * LANES
MESH = pl.DeviceIdType.MESH
UNITS = ((0, 0), (1, 1), (7, 0), (2, 1), (6, 0), (3, 1), (5, 0), (4, 1))
SLOTS = 4


def channel_tables():
    position = np.arange(PIECES * LANES)
    table = np.zeros((PIECES, 2, LANES, 2, 2, WIDTH))
    turned = np.zeros_like(table)
    for parity in range(2):
        m = position - HOP * parity
        inside = (m >= 0) & (m < C)
        hann = np.where(inside, (0.5 - 0.5 * np.cos(2 * np.pi * m / C)) / math.sqrt(3 * C / 8), 0.0)
        turns = (position[:, None] * np.arange(WIDTH)[None]) % C
        w = hann[:, None] * np.exp(-2j * np.pi * turns / C)
        for part, v in enumerate((w, 1j * w)):
            v = v.reshape(PIECES, LANES, WIDTH)
            table[:, part, :, parity, 0] = v.real
            table[:, part, :, parity, 1] = v.imag
            turned[:, part, :, parity, 0] = v.imag
            turned[:, part, :, parity, 1] = -v.real
    tables = np.stack([table, turned]).reshape(2, DEPTH, 64)
    tables = np.concatenate([tables, tables], axis=2)
    angle = 2 * np.pi * (np.arange(16)[:, None] * np.arange(16)[None] % 16) / 16
    turns = np.stack([np.cos(angle), np.sin(angle)])
    turns = np.broadcast_to(turns[..., None], (2, 16, 16, LANES))
    return tables.astype(np.float32), np.ascontiguousarray(turns).astype(np.float32)


def second_tables():
    frame = np.arange(LANES)
    bins = np.arange(LANES)
    out = []
    for parity in range(2):
        turns = ((2 * frame[:, None] + parity) * bins[None]) % P_SIZE
        angle = 2 * np.pi * turns / P_SIZE
        c, s = np.cos(angle) / 16.0, np.sin(angle) / 16.0
        out.append(np.concatenate([np.concatenate([c, -s], 1), np.concatenate([s, c], 1)], 0))
    full = np.stack(out).astype(np.float32)
    high = full.astype(jnp.bfloat16)
    low = (full - high.astype(np.float32)).astype(jnp.bfloat16)
    return np.stack([high, low])


def signs():
    channel = np.arange(LANES) % WIDTH
    frame = np.arange(LANES)
    return np.where((channel[:, None] * frame[None]) % 2 == 1, -1.0, 1.0).astype(np.float32)


def halves(value):
    high = value.astype(jnp.bfloat16)
    low = (value - high.astype(jnp.float32)).astype(jnp.bfloat16)
    return high, low


def dot(a, b):
    return lax.dot_general(a, b, (((1,), (0,)), ((), ())), preferred_element_type=jnp.float32)


def first_weights(tables, turns, weights):
    row = lax.axis_index("row")
    col = lax.axis_index("col")
    lane = lax.broadcasted_iota(jnp.int32, (16, LANES), 1)
    cosine = jnp.where(lane < 64, turns[0, row], turns[0, col])
    sinus = jnp.where(lane < 64, turns[1, row], turns[1, col])
    groups = DEPTH // 16
    shaped = tables[...].reshape(2, groups, 16, LANES)
    full = (shaped[0] * cosine[None] + shaped[1] * sinus[None]).reshape(DEPTH, LANES)
    high, low = halves(full)
    weights[:, :LANES] = high
    weights[:, LANES:] = low


def channelize(ordered, weights, sign, base):
    step = 512

    def block(i, _):
        start = pl.multiple_of(i * (2 * step), 2 * step)
        pieces = [ordered[pl.ds(start + j, step, stride=2), :] for j in range(2 * PIECES)]
        high, low = halves(jnp.concatenate(pieces, axis=1))
        wide = dot(high, weights[...])
        result = wide[:, :LANES] + wide[:, LANES:] + dot(low, weights[:, :LANES])
        for k in range(step // LANES):
            turned = result[k * LANES : (k + 1) * LANES].T * sign[...]
            base[pl.ds(i * (step // LANES) + k, LANES, stride=WINDOWS), :] = turned
        return 0

    lax.fori_loop(0, ROWS // step, block, 0)


def correlate(a, base, second, out):
    def tile(first, count):
        return base[pl.ds(pl.multiple_of(first * WINDOWS, WINDOWS), count * WINDOWS), :]

    sums = []
    for parity in range(2):
        lead_re = tile(parity * 32 + a, 1)[None]
        lead_im = tile(parity * 32 + 16 + a, 1)[None]
        trail_re = tile(64 + parity * 32, 16).reshape(WIDTH, WINDOWS, LANES)
        trail_im = tile(64 + parity * 32 + 16, 16).reshape(WIDTH, WINDOWS, LANES)
        real = (lead_re * trail_re + lead_im * trail_im).reshape(256, LANES)
        imag = (lead_im * trail_re - lead_re * trail_im).reshape(256, LANES)
        high, low = halves(jnp.concatenate([real, imag], axis=1))
        sums.append(dot(high, second[0, parity]) + dot(low, second[0, parity]) + dot(high, second[1, parity]))
    total = sums[0] + sums[1]
    rest = sums[0] - sums[1]
    for j, value in enumerate((total[:, :LANES], total[:, LANES:], rest[:, :LANES], rest[:, LANES:])):
        out[pl.ds(j, 256, stride=4), :] = value


def kernel(base, second, out, buffer, sems):
    def store(a, slot):
        place = pl.ds(pl.multiple_of(a * 1024, 1024), 1024)
        return pltpu.make_async_copy(buffer.at[slot], out.at[place], sems.at[slot])

    def step(a, _):
        slot = lax.rem(a, SLOTS)

        @pl.when(a >= SLOTS)
        def _():
            store(a, slot).wait()

        correlate(a, base, second, buffer.at[slot])
        store(a, slot).start()
        return 0

    lax.fori_loop(0, WIDTH, step, 0)
    for a in range(WIDTH - SLOTS, WIDTH):
        store(a, a % SLOTS).wait()


def spectra(base):
    whole = pl.BlockSpec(memory_space=pltpu.VMEM)
    return pl.pallas_call(
        kernel,
        out_shape=jax.ShapeDtypeStruct((WIDTH * 1024, LANES), jnp.float32),
        in_specs=[whole, whole],
        out_specs=pl.BlockSpec(memory_space=pl.ANY),
        scratch_shapes=[pltpu.VMEM((SLOTS, 1024, LANES), jnp.float32), pltpu.SemaphoreType.DMA((SLOTS,))],
    )(base, jnp.asarray(second_tables()))


def gather_kernel(
    own, tables_hbm, turns_hbm, sign_hbm, base, ordered, tables, turns, sign, weights,
    loaded, copied, z_send, z_recv, first_send, first_recv, second_send, second_recv, core_send, core_recv
):
    row = lax.axis_index("row")
    col = lax.axis_index("col")
    core = lax.rem(row, 2)
    x = lax.div(row, 4)
    y = lax.rem(lax.div(row, 2), 2) * 2 + lax.rem(col, 2)
    z = lax.div(col, 2)

    def moved(value, distance, length=4):
        return lax.rem(value + (distance + length), length) if distance else value

    def device(x, y, z, core):
        return (x * 4 + lax.div(y, 2) * 2 + core, z * 2 + lax.rem(y, 2))

    def at(half, first, second):
        px, py = ((first, second), (second, first))[half]
        return moved(x, px), moved(y, py)

    def beside(half, first, second):
        return device(*at(half, first, second), z, core)

    other = device(x, y, z, 1 - core)
    x_rows = [moved(x, d) * 1024 for d in range(4)]
    y_rows = [lax.div(moved(y, d), 2) * 512 + lax.rem(moved(y, d), 2) * 16 for d in range(4)]
    z_rows = [moved(z, d, 8) * 32 + core * 256 for d in range(8)]

    def chunk(unit, first, second):
        d, half = UNITS[unit]
        px, py = ((first, second), (second, first))[half]
        return ordered.at[pl.ds(pl.multiple_of(x_rows[px % 4] + y_rows[py % 4] + z_rows[d], 16), 16)]

    def send(ref, send_sem, recv_sem, to, source=None):
        pltpu.make_async_remote_copy(
            src_ref=ref if source is None else source,
            dst_ref=ref, send_sem=send_sem, recv_sem=recv_sem, device_id=to, device_id_type=MESH,
        ).start()

    def wait(chunks, sem):
        ref = ordered.at[pl.ds(0, 16 * chunks)]
        pltpu.make_async_copy(ref, ref, sem).wait()

    barrier = pltpu.get_barrier_semaphore()
    peers = [device(x, y, moved(z, d, 8), core) for d in range(1, 8)]
    peers += [beside(half, d, 0) for half in range(2) for d in range(1, 4)] + [other]
    for peer in peers:
        pl.semaphore_signal(barrier, inc=1, device_id=peer, device_id_type=MESH)
    local_copy = pltpu.make_async_copy(own, chunk(0, 0, 0), copied)
    local_copy.start()
    loads = [
        pltpu.make_async_copy(source, target, loaded.at[i])
        for i, (source, target) in enumerate(((tables_hbm, tables), (turns_hbm, turns), (sign_hbm, sign)))
    ]
    for load in loads:
        load.start()
    ordered[2 * ROWS :, :] = jnp.zeros((8, LANES), jnp.float32)
    pl.semaphore_wait(barrier, len(peers))

    def to_second(unit, j):
        half = UNITS[unit][1]
        for e in (1, 3, 2):
            send(
                chunk(unit, j, 0), second_send.at[unit], second_recv.at[unit * 3 + e - 1], beside(half, 0, e)
            )

    def to_core(unit, e):
        for j in range(4):
            send(chunk(unit, j, e), core_send.at[unit], core_recv.at[unit], other)

    def begin(unit):
        half = UNITS[unit][1]
        for e in (1, 3, 2):
            send(chunk(unit, 0, 0), first_send.at[unit], first_recv.at[unit], beside(half, e, 0))
        to_second(unit, 0)

    def z_done(unit):
        wait(1, z_recv.at[unit - 1])
        begin(unit)

    def first_done(unit):
        wait(3, first_recv.at[unit])
        for j in (1, 3, 2):
            to_second(unit, j)
        to_core(unit, 0)

    def second_done(unit):
        for e in (1, 3, 2):
            wait(4, second_recv.at[unit * 3 + e - 1])
            to_core(unit, -e)

    mine = x_rows[0] + y_rows[0] + z_rows[0]
    for unit in range(1, 8):
        d = UNITS[unit][0]
        ref = ordered.at[pl.ds(pl.multiple_of(mine, 16), 16)]
        send(ref, z_send.at[unit - 1], z_recv.at[unit - 1], device(x, y, moved(z, -d, 8), core), own)
    local_copy.wait()
    begin(0)
    for load in loads:
        load.wait()
    first_weights(tables, turns, weights)
    z_done(1)
    z_done(2)
    first_done(0)
    for unit in range(3, 8):
        z_done(unit)
    first_done(1)
    first_done(2)
    second_done(0)
    for unit in range(3, 8):
        first_done(unit)
    for unit in range(1, 8):
        second_done(unit)
    for unit in range(8):
        wait(16, core_recv.at[unit])
    channelize(ordered, weights, sign, base)
    for unit in range(8):
        if unit:
            wait(1, z_send.at[unit - 1])
        wait(3, first_send.at[unit])
        wait(12, second_send.at[unit])
        wait(16, core_send.at[unit])


def gather(tiles):
    def sems(count):
        return pltpu.SemaphoreType.DMA((count,))

    tables, turns = channel_tables()
    anywhere = pl.BlockSpec(memory_space=pl.ANY)
    return pl.pallas_call(
        gather_kernel,
        out_shape=jax.ShapeDtypeStruct((LANES * WINDOWS, LANES), jnp.float32),
        in_specs=[pl.BlockSpec(memory_space=pltpu.VMEM), anywhere, anywhere, anywhere],
        out_specs=pl.BlockSpec(memory_space=pltpu.VMEM),
        scratch_shapes=[
            pltpu.VMEM((2 * ROWS + 8, LANES), jnp.float32),
            pltpu.VMEM(tables.shape, jnp.float32),
            pltpu.VMEM(turns.shape, jnp.float32),
            pltpu.VMEM((LANES, LANES), jnp.float32),
            pltpu.VMEM((DEPTH, 2 * LANES), jnp.bfloat16),
            sems(3),
            pltpu.SemaphoreType.DMA,
            sems(7), sems(7), sems(8), sems(8), sems(8), sems(24), sems(8), sems(8),
        ],
        compiler_params=pltpu.CompilerParams(collective_id=0, has_side_effects=True),
    )(tiles, jnp.asarray(tables), jnp.asarray(turns), jnp.asarray(signs()))


def local(record):
    tiles = record.reshape(2, 8, LANES).transpose(1, 0, 2).reshape(16, LANES)
    result = spectra(gather(tiles))
    result = result.reshape(WIDTH, WIDTH, WINDOWS, 2, 2, LANES)
    result = result.transpose(0, 1, 2, 4, 3, 5)
    return result.reshape(WIDTH, WIDTH, WINDOWS, 2, 2 * LANES)


def solution(mesh):
    return jax.shard_map(
        local,
        mesh=mesh,
        in_specs=(P(None, ("row", "col")),),
        out_specs=P("row", "col", None, None, None),
        check_vma=False,
    )
```

```python
import math

import jax
import jax.numpy as jnp
import numpy as np
from jax import lax
from jax.experimental import pallas as pl
from jax.experimental.pallas import tpu as pltpu
from jax.sharding import PartitionSpec as P

C = 256
P_SIZE = 256
HOP = 64
LANES = 128
WIDTH = 16
WINDOWS = 16
ROWS = 2048
PIECES = 3
DEPTH = PIECES * 2 * LANES
MESH = pl.DeviceIdType.MESH
UNITS = ((0, 0), (1, 1), (7, 0), (2, 1), (6, 0), (3, 1), (5, 0), (4, 1))
SLOTS = 4
VMEM_LIMIT = 16 * 2**20


def cosine_series():
    nodes = 0.5 - 0.5 * np.cos(np.pi * (np.arange(64) + 0.5) / 64)
    fit = np.polynomial.chebyshev.Chebyshev.fit(nodes, -np.cos(np.pi * np.sqrt(nodes)), 8, domain=[0, 1])
    return [float(c) for c in fit.convert(kind=np.polynomial.Polynomial).coef]


SERIES = cosine_series()


def cosine(turns):
    w = ((turns & 255) - 128).astype(jnp.float32) * (1.0 / 128)
    square = w * w
    result = jnp.full(w.shape, SERIES[-1], jnp.float32)
    for c in SERIES[-2::-1]:
        result = result * square + c
    return result


def grid_of(dim):
    return lax.broadcasted_iota(jnp.int32, (LANES, LANES), dim)


def halves(value):
    high = value.astype(jnp.bfloat16)
    low = (value - high.astype(jnp.float32)).astype(jnp.bfloat16)
    return high, low


def dot(a, b):
    return lax.dot_general(a, b, (((1,), (0,)), ((), ())), preferred_element_type=jnp.float32)


def first_weights(weights):
    column = grid_of(1)
    block = jnp.where(column < 64, lax.axis_index("row"), lax.axis_index("col"))
    channel = block * WIDTH + column % WIDTH
    odd = (column // 32) % 2
    imag = (column // 16) % 2
    for piece in range(PIECES):
        position = grid_of(0) + piece * LANES
        m = position - HOP * odd
        window = (0.5 - 0.5 * cosine(m)) * (1.0 / math.sqrt(3 * C / 8))
        window = jnp.where((m >= 0) & (m < C), window, 0.0)
        for part in range(2):
            shift = 64 * imag if part == 0 else 192 * (1 - imag)
            high, low = halves(window * cosine(channel * position + shift))
            start = (2 * piece + part) * LANES
            weights[start : start + LANES, :LANES] = high
            weights[start : start + LANES, LANES:] = low


def second_tables(second):
    for parity in range(2):
        turns = (2 * grid_of(0) + parity) * grid_of(1)
        plain = cosine(turns) * (1.0 / 16)
        for part in range(2):
            for imag in range(2):
                value = plain if part == imag else cosine(turns + (64 if imag else 192)) * (1.0 / 16)
                high, low = halves(value)
                rows = slice(part * LANES, (part + 1) * LANES)
                columns = slice(imag * LANES, (imag + 1) * LANES)
                second[0, parity, rows, columns] = high
                second[1, parity, rows, columns] = low


def channelize(ordered, weights, base):
    step = 512
    sign = (1 - 2 * (grid_of(0) & grid_of(1) & 1)).astype(jnp.float32)

    def block(i, _):
        start = pl.multiple_of(i * (2 * step), 2 * step)
        pieces = [ordered[pl.ds(start + j, step, stride=2), :] for j in range(2 * PIECES)]
        high, low = halves(jnp.concatenate(pieces, axis=1))
        wide = dot(high, weights[...])
        result = wide[:, :LANES] + wide[:, LANES:] + dot(low, weights[:, :LANES])
        for k in range(step // LANES):
            turned = result[k * LANES : (k + 1) * LANES].T * sign
            base[pl.ds(i * (step // LANES) + k, LANES, stride=WINDOWS), :] = turned
        return 0

    lax.fori_loop(0, ROWS // step, block, 0)


def correlate(a, base, second, out):
    def tile(first, count):
        return base[pl.ds(pl.multiple_of(first * WINDOWS, WINDOWS), count * WINDOWS), :]

    sums = []
    for parity in range(2):
        lead_re = tile(parity * 32 + a, 1)[None]
        lead_im = tile(parity * 32 + 16 + a, 1)[None]
        trail_re = tile(64 + parity * 32, 16).reshape(WIDTH, WINDOWS, LANES)
        trail_im = tile(64 + parity * 32 + 16, 16).reshape(WIDTH, WINDOWS, LANES)
        real = (lead_re * trail_re + lead_im * trail_im).reshape(256, LANES)
        imag = (lead_im * trail_re - lead_re * trail_im).reshape(256, LANES)
        high, low = halves(jnp.concatenate([real, imag], axis=1))
        sums.append(dot(high, second[0, parity]) + dot(low, second[0, parity]) + dot(high, second[1, parity]))
    total = sums[0] + sums[1]
    rest = sums[0] - sums[1]
    for j, value in enumerate((total[:, :LANES], total[:, LANES:], rest[:, :LANES], rest[:, LANES:])):
        out[pl.ds(j, 256, stride=4), :] = value


def kernel(base, second, out, buffer, sems):
    def store(a, slot):
        place = pl.ds(pl.multiple_of(a * 1024, 1024), 1024)
        return pltpu.make_async_copy(buffer.at[slot], out.at[place], sems.at[slot])

    def step(a, _):
        slot = lax.rem(a, SLOTS)

        @pl.when(a >= SLOTS)
        def _():
            store(a, slot).wait()

        correlate(a, base, second, buffer.at[slot])
        store(a, slot).start()
        return 0

    lax.fori_loop(0, WIDTH, step, 0)
    for a in range(WIDTH - SLOTS, WIDTH):
        store(a, a % SLOTS).wait()


def spectra(base, second):
    whole = pl.BlockSpec(memory_space=pltpu.VMEM)
    return pl.pallas_call(
        kernel,
        out_shape=jax.ShapeDtypeStruct((WIDTH * 1024, LANES), jnp.float32),
        in_specs=[whole, whole],
        out_specs=pl.BlockSpec(memory_space=pl.ANY),
        scratch_shapes=[pltpu.VMEM((SLOTS, 1024, LANES), jnp.float32), pltpu.SemaphoreType.DMA((SLOTS,))],
        compiler_params=pltpu.CompilerParams(vmem_limit_bytes=VMEM_LIMIT),
    )(base, second)


def gather_kernel(
    own, base, second, ordered, weights, copied,
    z_send, z_recv, first_send, first_recv, second_send, second_recv, core_send, core_recv
):
    row = lax.axis_index("row")
    col = lax.axis_index("col")
    core = lax.rem(row, 2)
    x = lax.div(row, 4)
    y = lax.rem(lax.div(row, 2), 2) * 2 + lax.rem(col, 2)
    z = lax.div(col, 2)

    def moved(value, distance, length=4):
        return lax.rem(value + (distance + length), length) if distance else value

    def device(x, y, z, core):
        return (x * 4 + lax.div(y, 2) * 2 + core, z * 2 + lax.rem(y, 2))

    def at(half, first, second):
        px, py = ((first, second), (second, first))[half]
        return moved(x, px), moved(y, py)

    def beside(half, first, second):
        return device(*at(half, first, second), z, core)

    other = device(x, y, z, 1 - core)
    x_rows = [moved(x, d) * 1024 for d in range(4)]
    y_rows = [lax.div(moved(y, d), 2) * 512 + lax.rem(moved(y, d), 2) * 16 for d in range(4)]
    z_rows = [moved(z, d, 8) * 32 + core * 256 for d in range(8)]

    def chunk(unit, first, second):
        d, half = UNITS[unit]
        px, py = ((first, second), (second, first))[half]
        return ordered.at[pl.ds(pl.multiple_of(x_rows[px % 4] + y_rows[py % 4] + z_rows[d], 16), 16)]

    def send(ref, send_sem, recv_sem, to):
        pltpu.make_async_remote_copy(
            src_ref=ref, dst_ref=ref, send_sem=send_sem, recv_sem=recv_sem, device_id=to, device_id_type=MESH
        ).start()

    def wait(chunks, sem):
        ref = ordered.at[pl.ds(0, 16 * chunks)]
        pltpu.make_async_copy(ref, ref, sem).wait()

    barrier = pltpu.get_barrier_semaphore()
    peers = [device(x, y, moved(z, d, 8), core) for d in range(1, 8)]
    peers += [beside(half, d, 0) for half in range(2) for d in range(1, 4)] + [other]
    for peer in peers:
        pl.semaphore_signal(barrier, inc=1, device_id=peer, device_id_type=MESH)
    local_copy = pltpu.make_async_copy(own, chunk(0, 0, 0), copied)
    local_copy.start()
    ordered[2 * ROWS :, :] = jnp.zeros((8, LANES), jnp.float32)
    pl.semaphore_wait(barrier, len(peers))

    def to_second(unit, j):
        half = UNITS[unit][1]
        for e in (1, 3, 2):
            send(
                chunk(unit, j, 0), second_send.at[unit], second_recv.at[unit * 3 + e - 1], beside(half, 0, e)
            )

    def to_core(unit, e):
        for j in range(4):
            send(chunk(unit, j, e), core_send.at[unit], core_recv.at[unit], other)

    def begin(unit):
        half = UNITS[unit][1]
        for e in (1, 3, 2):
            send(chunk(unit, 0, 0), first_send.at[unit], first_recv.at[unit], beside(half, e, 0))
        to_second(unit, 0)

    def z_done(unit):
        wait(1, z_recv.at[unit - 1])
        begin(unit)

    def first_done(unit):
        wait(3, first_recv.at[unit])
        for j in (1, 3, 2):
            to_second(unit, j)
        to_core(unit, 0)

    def second_done(unit):
        for e in (1, 3, 2):
            wait(4, second_recv.at[unit * 3 + e - 1])
            to_core(unit, -e)

    mine = x_rows[0] + y_rows[0] + z_rows[0]
    local_copy.wait()
    for unit in range(1, 8):
        d = UNITS[unit][0]
        ref = ordered.at[pl.ds(pl.multiple_of(mine, 16), 16)]
        send(ref, z_send.at[unit - 1], z_recv.at[unit - 1], device(x, y, moved(z, -d, 8), core))
    begin(0)
    first_weights(weights)
    z_done(1)
    z_done(2)
    first_done(0)
    for unit in range(3, 8):
        z_done(unit)
    second_tables(second)
    first_done(1)
    first_done(2)
    second_done(0)
    for unit in range(3, 8):
        first_done(unit)
    for unit in range(1, 8):
        second_done(unit)
    for unit in range(8):
        wait(16, core_recv.at[unit])
    channelize(ordered, weights, base)
    for unit in range(8):
        if unit:
            wait(1, z_send.at[unit - 1])
        wait(3, first_send.at[unit])
        wait(12, second_send.at[unit])
        wait(16, core_send.at[unit])


def gather(tiles):
    def sems(count):
        return pltpu.SemaphoreType.DMA((count,))

    far = pl.BlockSpec(memory_space=pl.ANY)
    near = pl.BlockSpec(memory_space=pltpu.VMEM)
    return pl.pallas_call(
        gather_kernel,
        out_shape=[
            jax.ShapeDtypeStruct((LANES * WINDOWS, LANES), jnp.float32),
            jax.ShapeDtypeStruct((2, 2, 256, 256), jnp.bfloat16),
        ],
        in_specs=[far],
        out_specs=[near] * 2,
        scratch_shapes=[
            pltpu.VMEM((2 * ROWS + 8, LANES), jnp.float32),
            pltpu.VMEM((DEPTH, 2 * LANES), jnp.bfloat16),
            pltpu.SemaphoreType.DMA,
            sems(7), sems(7), sems(8), sems(8), sems(8), sems(24), sems(8), sems(8),
        ],
        compiler_params=pltpu.CompilerParams(
            collective_id=0, has_side_effects=True, vmem_limit_bytes=VMEM_LIMIT
        ),
    )(tiles)


def local(record):
    tiles = record.reshape(2, 8, LANES).transpose(1, 0, 2).reshape(16, LANES)
    result = spectra(*gather(tiles))
    result = result.reshape(WIDTH, WIDTH, WINDOWS, 2, 2, LANES)
    result = result.transpose(0, 1, 2, 4, 3, 5)
    return result.reshape(WIDTH, WIDTH, WINDOWS, 2, 2 * LANES)


def solution(mesh):
    return jax.shard_map(
        local,
        mesh=mesh,
        in_specs=(P(None, ("row", "col")),),
        out_specs=P("row", "col", None, None, None),
        check_vma=False,
    )
```

```python
import math

import jax
import jax.numpy as jnp
import numpy as np
from jax import lax
from jax.experimental import pallas as pl
from jax.experimental.pallas import tpu as pltpu
from jax.sharding import PartitionSpec as P

C = 256
P_SIZE = 256
HOP = 64
LANES = 128
WIDTH = 16
WINDOWS = 16
ROWS = 2048
PIECES = 3
DEPTH = PIECES * 2 * LANES
MESH = pl.DeviceIdType.MESH
UNITS = ((0, 0), (1, 1), (7, 0), (2, 1), (6, 0), (3, 1), (5, 0), (4, 1))
SLOTS = 4
GROUP = 4
VMEM_LIMIT = 16 * 2**20


def cosine_series():
    nodes = 0.5 - 0.5 * np.cos(np.pi * (np.arange(64) + 0.5) / 64)
    fit = np.polynomial.chebyshev.Chebyshev.fit(nodes, -np.cos(np.pi * np.sqrt(nodes)), 8, domain=[0, 1])
    return [float(c) for c in fit.convert(kind=np.polynomial.Polynomial).coef]


SERIES = cosine_series()


def cosine(turns):
    w = ((turns & 255) - 128).astype(jnp.float32) * (1.0 / 128)
    square = w * w
    result = jnp.full(w.shape, SERIES[-1], jnp.float32)
    for c in SERIES[-2::-1]:
        result = result * square + c
    return result


def grid_of(dim):
    return lax.broadcasted_iota(jnp.int32, (LANES, LANES), dim)


def halves(value):
    high = value.astype(jnp.bfloat16)
    low = (value - high.astype(jnp.float32)).astype(jnp.bfloat16)
    return high, low


def dot(a, b):
    return lax.dot_general(a, b, (((1,), (0,)), ((), ())), preferred_element_type=jnp.float32)


def first_weights(weights):
    column = grid_of(1)
    block = jnp.where(column < 64, lax.axis_index("row"), lax.axis_index("col"))
    channel = block * WIDTH + column % WIDTH
    odd = (column // 32) % 2
    imag = (column // 16) % 2
    for piece in range(PIECES):
        position = grid_of(0) + piece * LANES
        m = position - HOP * odd
        window = (0.5 - 0.5 * cosine(m)) * (1.0 / math.sqrt(3 * C / 8))
        window = jnp.where((m >= 0) & (m < C), window, 0.0)
        for part in range(2):
            shift = 64 * imag if part == 0 else 192 * (1 - imag)
            high, low = halves(window * cosine(channel * position + shift))
            start = (2 * piece + part) * LANES
            weights[start : start + LANES, :LANES] = high
            weights[start : start + LANES, LANES:] = low


def second_tables(second):
    for parity in range(2):
        turns = (2 * grid_of(0) + parity) * grid_of(1)
        plain = cosine(turns) * (1.0 / 16)
        for part in range(2):
            for imag in range(2):
                value = plain if part == imag else cosine(turns + (64 if imag else 192)) * (1.0 / 16)
                high, low = halves(value)
                rows = slice(part * LANES, (part + 1) * LANES)
                columns = slice(imag * LANES, (imag + 1) * LANES)
                second[0, parity, rows, columns] = high
                second[1, parity, rows, columns] = low


def channelize(ordered, weights, base):
    step = 512
    sign = (1 - 2 * (grid_of(0) & grid_of(1) & 1)).astype(jnp.float32)

    def block(i, _):
        start = pl.multiple_of(i * (2 * step), 2 * step)
        pieces = [ordered[pl.ds(start + j, step, stride=2), :] for j in range(2 * PIECES)]
        high, low = halves(jnp.concatenate(pieces, axis=1))
        wide = dot(high, weights[...])
        result = wide[:, :LANES] + wide[:, LANES:] + dot(low, weights[:, :LANES])
        for k in range(step // LANES):
            turned = result[k * LANES : (k + 1) * LANES].T * sign
            base[pl.ds(i * (step // LANES) + k, LANES, stride=WINDOWS), :] = turned
        return 0

    lax.fori_loop(0, ROWS // step, block, 0)


def correlate(step, base, second, out):
    count = GROUP * 256

    def tile(first, channels):
        return base[pl.ds(pl.multiple_of(first * WINDOWS, WINDOWS), channels * WINDOWS), :]

    sums = []
    for parity in range(2):
        lead_re = tile(parity * 32 + step * GROUP, GROUP).reshape(GROUP, 1, WINDOWS, LANES)
        lead_im = tile(parity * 32 + 16 + step * GROUP, GROUP).reshape(GROUP, 1, WINDOWS, LANES)
        trail_re = tile(64 + parity * 32, 16).reshape(1, WIDTH, WINDOWS, LANES)
        trail_im = tile(64 + parity * 32 + 16, 16).reshape(1, WIDTH, WINDOWS, LANES)
        real = (lead_re * trail_re + lead_im * trail_im).reshape(count, LANES)
        imag = (lead_im * trail_re - lead_re * trail_im).reshape(count, LANES)
        high, low = halves(jnp.concatenate([real, imag], axis=1))
        both = dot(jnp.concatenate([high, low], axis=0), second[0, parity])
        sums.append(both[:count] + both[count:] + dot(high, second[1, parity]))
    total = sums[0] + sums[1]
    rest = sums[0] - sums[1]
    for j, value in enumerate((total[:, :LANES], total[:, LANES:], rest[:, :LANES], rest[:, LANES:])):
        out[pl.ds(j, count, stride=4), :] = value


def kernel(base, second, out, buffer, sems):
    size = GROUP * 1024
    steps = WIDTH // GROUP

    def store(a, slot):
        place = pl.ds(pl.multiple_of(a * size, size), size)
        return pltpu.make_async_copy(buffer.at[slot], out.at[place], sems.at[slot])

    def step(a, _):
        slot = lax.rem(a, SLOTS)

        @pl.when(a >= SLOTS)
        def _():
            store(a, slot).wait()

        correlate(a, base, second, buffer.at[slot])
        store(a, slot).start()
        return 0

    lax.fori_loop(0, steps, step, 0)
    for a in range(steps - SLOTS, steps):
        store(a, a % SLOTS).wait()


def spectra(base, second):
    whole = pl.BlockSpec(memory_space=pltpu.VMEM)
    return pl.pallas_call(
        kernel,
        out_shape=jax.ShapeDtypeStruct((WIDTH * 1024, LANES), jnp.float32),
        in_specs=[whole, whole],
        out_specs=pl.BlockSpec(memory_space=pl.ANY),
        scratch_shapes=[pltpu.VMEM((SLOTS, GROUP * 1024, LANES), jnp.float32), pltpu.SemaphoreType.DMA((SLOTS,))],
        compiler_params=pltpu.CompilerParams(vmem_limit_bytes=VMEM_LIMIT),
    )(base, second)


def gather_kernel(
    own, base, second, ordered, weights, copied,
    z_send, z_recv, first_send, first_recv, second_send, second_recv, core_send, core_recv
):
    row = lax.axis_index("row")
    col = lax.axis_index("col")
    core = lax.rem(row, 2)
    x = lax.div(row, 4)
    y = lax.rem(lax.div(row, 2), 2) * 2 + lax.rem(col, 2)
    z = lax.div(col, 2)

    def moved(value, distance, length=4):
        return lax.rem(value + (distance + length), length) if distance else value

    def device(x, y, z, core):
        return (x * 4 + lax.div(y, 2) * 2 + core, z * 2 + lax.rem(y, 2))

    def at(half, first, second):
        px, py = ((first, second), (second, first))[half]
        return moved(x, px), moved(y, py)

    def beside(half, first, second):
        return device(*at(half, first, second), z, core)

    other = device(x, y, z, 1 - core)
    x_rows = [moved(x, d) * 1024 for d in range(4)]
    y_rows = [lax.div(moved(y, d), 2) * 512 + lax.rem(moved(y, d), 2) * 16 for d in range(4)]
    z_rows = [moved(z, d, 8) * 32 + core * 256 for d in range(8)]

    def chunk(unit, first, second):
        d, half = UNITS[unit]
        px, py = ((first, second), (second, first))[half]
        return ordered.at[pl.ds(pl.multiple_of(x_rows[px % 4] + y_rows[py % 4] + z_rows[d], 16), 16)]

    def send(ref, send_sem, recv_sem, to):
        pltpu.make_async_remote_copy(
            src_ref=ref, dst_ref=ref, send_sem=send_sem, recv_sem=recv_sem, device_id=to, device_id_type=MESH
        ).start()

    def wait(chunks, sem):
        ref = ordered.at[pl.ds(0, 16 * chunks)]
        pltpu.make_async_copy(ref, ref, sem).wait()

    barrier = pltpu.get_barrier_semaphore()
    peers = [device(x, y, moved(z, d, 8), core) for d in range(1, 8)]
    peers += [beside(half, d, 0) for half in range(2) for d in range(1, 4)] + [other]
    for peer in peers:
        pl.semaphore_signal(barrier, inc=1, device_id=peer, device_id_type=MESH)
    local_copy = pltpu.make_async_copy(own, chunk(0, 0, 0), copied)
    local_copy.start()
    ordered[2 * ROWS :, :] = jnp.zeros((8, LANES), jnp.float32)
    pl.semaphore_wait(barrier, len(peers))

    def to_second(unit, j):
        half = UNITS[unit][1]
        for e in (1, 3, 2):
            send(
                chunk(unit, j, 0), second_send.at[unit], second_recv.at[unit * 3 + e - 1], beside(half, 0, e)
            )

    def to_core(unit, e):
        for j in range(4):
            send(chunk(unit, j, e), core_send.at[unit], core_recv.at[unit], other)

    def begin(unit):
        half = UNITS[unit][1]
        for e in (1, 3, 2):
            send(chunk(unit, 0, 0), first_send.at[unit], first_recv.at[unit], beside(half, e, 0))
        to_second(unit, 0)

    def z_done(unit):
        wait(1, z_recv.at[unit - 1])
        begin(unit)

    def first_done(unit):
        wait(3, first_recv.at[unit])
        for j in (1, 3, 2):
            to_second(unit, j)
        to_core(unit, 0)

    def second_done(unit):
        for e in (1, 3, 2):
            wait(4, second_recv.at[unit * 3 + e - 1])
            to_core(unit, -e)

    mine = x_rows[0] + y_rows[0] + z_rows[0]
    local_copy.wait()
    for unit in range(1, 8):
        d = UNITS[unit][0]
        ref = ordered.at[pl.ds(pl.multiple_of(mine, 16), 16)]
        send(ref, z_send.at[unit - 1], z_recv.at[unit - 1], device(x, y, moved(z, -d, 8), core))
    begin(0)
    first_weights(weights)
    z_done(1)
    z_done(2)
    first_done(0)
    for unit in range(3, 8):
        z_done(unit)
    second_tables(second)
    first_done(1)
    first_done(2)
    second_done(0)
    for unit in range(3, 8):
        first_done(unit)
    for unit in range(1, 8):
        second_done(unit)
    for unit in range(8):
        wait(16, core_recv.at[unit])
    channelize(ordered, weights, base)
    for unit in range(8):
        if unit:
            wait(1, z_send.at[unit - 1])
        wait(3, first_send.at[unit])
        wait(12, second_send.at[unit])
        wait(16, core_send.at[unit])


def gather(tiles):
    def sems(count):
        return pltpu.SemaphoreType.DMA((count,))

    far = pl.BlockSpec(memory_space=pltpu.HBM)
    near = pl.BlockSpec(memory_space=pltpu.VMEM)
    return pl.pallas_call(
        gather_kernel,
        out_shape=[
            jax.ShapeDtypeStruct((LANES * WINDOWS, LANES), jnp.float32),
            jax.ShapeDtypeStruct((2, 2, 256, 256), jnp.bfloat16),
        ],
        in_specs=[far],
        out_specs=[near] * 2,
        scratch_shapes=[
            pltpu.VMEM((2 * ROWS + 8, LANES), jnp.float32),
            pltpu.VMEM((DEPTH, 2 * LANES), jnp.bfloat16),
            pltpu.SemaphoreType.DMA,
            sems(7), sems(7), sems(8), sems(8), sems(8), sems(24), sems(8), sems(8),
        ],
        compiler_params=pltpu.CompilerParams(
            collective_id=0, has_side_effects=True, vmem_limit_bytes=VMEM_LIMIT
        ),
    )(tiles)


def local(record):
    tiles = record.reshape(2, 8, LANES).transpose(1, 0, 2).reshape(16, LANES)
    tiles = pltpu.with_memory_space_constraint(tiles, pltpu.HBM)
    result = spectra(*gather(tiles))
    result = result.reshape(WIDTH, WIDTH, WINDOWS, 2, 2, LANES)
    result = result.transpose(0, 1, 2, 4, 3, 5)
    return result.reshape(WIDTH, WIDTH, WINDOWS, 2, 2 * LANES)


def solution(mesh):
    return jax.shard_map(
        local,
        mesh=mesh,
        in_specs=(P(None, ("row", "col")),),
        out_specs=P("row", "col", None, None, None),
        check_vma=False,
    )
```

```python
import math

import jax
import jax.numpy as jnp
import numpy as np
from jax import lax
from jax.experimental import pallas as pl
from jax.experimental.pallas import tpu as pltpu
from jax.sharding import PartitionSpec as P

C = 256
P_SIZE = 256
HOP = 64
LANES = 128
WIDTH = 16
WINDOWS = 16
ROWS = 2048
PIECES = 3
DEPTH = PIECES * 2 * LANES
MESH = pl.DeviceIdType.MESH
UNITS = ((0, 0), (1, 1), (7, 0), (2, 1), (6, 0), (3, 1), (5, 0), (4, 1))
SLOTS = 4
GROUP = 4
VMEM_LIMIT = 16 * 2**20


def cosine_series():
    nodes = 0.5 - 0.5 * np.cos(np.pi * (np.arange(64) + 0.5) / 64)
    fit = np.polynomial.chebyshev.Chebyshev.fit(nodes, -np.cos(np.pi * np.sqrt(nodes)), 8, domain=[0, 1])
    return [float(c) for c in fit.convert(kind=np.polynomial.Polynomial).coef]


SERIES = cosine_series()


def cosine(turns):
    w = ((turns & 255) - 128).astype(jnp.float32) * (1.0 / 128)
    square = w * w
    result = jnp.full(w.shape, SERIES[-1], jnp.float32)
    for c in SERIES[-2::-1]:
        result = result * square + c
    return result


def grid_of(dim):
    return lax.broadcasted_iota(jnp.int32, (LANES, LANES), dim)


def halves(value):
    high = value.astype(jnp.bfloat16)
    low = (value - high.astype(jnp.float32)).astype(jnp.bfloat16)
    return high, low


def dot(a, b):
    return lax.dot_general(a, b, (((1,), (0,)), ((), ())), preferred_element_type=jnp.float32)


def first_weights(weights):
    column = grid_of(1)
    block = jnp.where(column < 64, lax.axis_index("row"), lax.axis_index("col"))
    channel = block * WIDTH + column % WIDTH
    odd = (column // 32) % 2
    imag = (column // 16) % 2
    for piece in range(PIECES):
        position = grid_of(0) + piece * LANES
        m = position - HOP * odd
        window = (0.5 - 0.5 * cosine(m)) * (1.0 / math.sqrt(3 * C / 8))
        window = jnp.where((m >= 0) & (m < C), window, 0.0)
        for part in range(2):
            shift = 64 * imag if part == 0 else 192 * (1 - imag)
            high, low = halves(window * cosine(channel * position + shift))
            start = (2 * piece + part) * LANES
            weights[start : start + LANES, :LANES] = high
            weights[start : start + LANES, LANES:] = low


def second_tables(second):
    for parity in range(2):
        turns = (2 * grid_of(0) + parity) * grid_of(1)
        plain = cosine(turns) * (1.0 / 16)
        for part in range(2):
            for imag in range(2):
                value = plain if part == imag else cosine(turns + (64 if imag else 192)) * (1.0 / 16)
                high, low = halves(value)
                rows = slice(part * LANES, (part + 1) * LANES)
                columns = slice(imag * LANES, (imag + 1) * LANES)
                second[0, parity, rows, columns] = high
                second[1, parity, rows, columns] = low


def channelize(ordered, weights, base):
    step = 1024
    sign = (1 - 2 * (grid_of(0) & grid_of(1) & 1)).astype(jnp.float32)

    def block(i, _):
        start = pl.multiple_of(i * (2 * step), 2 * step)
        pieces = [ordered[pl.ds(start + j, step, stride=2), :] for j in range(2 * PIECES)]
        high, low = halves(jnp.concatenate(pieces, axis=1))
        wide = dot(jnp.concatenate([high, low], axis=0), weights[...])
        result = wide[:step, :LANES] + wide[:step, LANES:] + wide[step:, :LANES]
        for k in range(step // LANES):
            turned = result[k * LANES : (k + 1) * LANES].T * sign
            base[pl.ds(i * (step // LANES) + k, LANES, stride=WINDOWS), :] = turned
        return 0

    lax.fori_loop(0, ROWS // step, block, 0)


def correlate(step, base, second, out):
    count = GROUP * 256

    def tile(first, channels):
        return base[pl.ds(pl.multiple_of(first * WINDOWS, WINDOWS), channels * WINDOWS), :]

    sums = []
    for parity in range(2):
        lead_re = tile(parity * 32 + step * GROUP, GROUP).reshape(GROUP, 1, WINDOWS, LANES)
        lead_im = tile(parity * 32 + 16 + step * GROUP, GROUP).reshape(GROUP, 1, WINDOWS, LANES)
        trail_re = tile(64 + parity * 32, 16).reshape(1, WIDTH, WINDOWS, LANES)
        trail_im = tile(64 + parity * 32 + 16, 16).reshape(1, WIDTH, WINDOWS, LANES)
        real = (lead_re * trail_re + lead_im * trail_im).reshape(count, LANES)
        imag = (lead_im * trail_re - lead_re * trail_im).reshape(count, LANES)
        high, low = halves(jnp.concatenate([real, imag], axis=1))
        both = dot(jnp.concatenate([high, low], axis=0), second[0, parity])
        sums.append(both[:count] + both[count:] + dot(high, second[1, parity]))
    total = sums[0] + sums[1]
    rest = sums[0] - sums[1]
    for j, value in enumerate((total[:, :LANES], total[:, LANES:], rest[:, :LANES], rest[:, LANES:])):
        out[pl.ds(j, count, stride=4), :] = value


def kernel(base, second, out, buffer, sems):
    size = GROUP * 1024
    steps = WIDTH // GROUP

    def store(a, slot):
        place = pl.ds(pl.multiple_of(a * size, size), size)
        return pltpu.make_async_copy(buffer.at[slot], out.at[place], sems.at[slot])

    def step(a, _):
        slot = lax.rem(a, SLOTS)

        @pl.when(a >= SLOTS)
        def _():
            store(a, slot).wait()

        correlate(a, base, second, buffer.at[slot])
        store(a, slot).start()
        return 0

    lax.fori_loop(0, steps, step, 0, unroll=True)
    for a in range(steps - SLOTS, steps):
        store(a, a % SLOTS).wait()


def spectra(base, second):
    whole = pl.BlockSpec(memory_space=pltpu.VMEM)
    return pl.pallas_call(
        kernel,
        out_shape=jax.ShapeDtypeStruct((WIDTH * 1024, LANES), jnp.float32),
        in_specs=[whole, whole],
        out_specs=pl.BlockSpec(memory_space=pl.ANY),
        scratch_shapes=[pltpu.VMEM((SLOTS, GROUP * 1024, LANES), jnp.float32), pltpu.SemaphoreType.DMA((SLOTS,))],
        compiler_params=pltpu.CompilerParams(vmem_limit_bytes=VMEM_LIMIT),
    )(base, second)


def gather_kernel(
    own, base, second, ordered, weights, copied,
    z_send, z_recv, first_send, first_recv, second_send, second_recv, core_send, core_recv
):
    row = lax.axis_index("row")
    col = lax.axis_index("col")
    core = lax.rem(row, 2)
    x = lax.div(row, 4)
    y = lax.rem(lax.div(row, 2), 2) * 2 + lax.rem(col, 2)
    z = lax.div(col, 2)

    def moved(value, distance, length=4):
        return lax.rem(value + (distance + length), length) if distance else value

    def device(x, y, z, core):
        return (x * 4 + lax.div(y, 2) * 2 + core, z * 2 + lax.rem(y, 2))

    def at(half, first, second):
        px, py = ((first, second), (second, first))[half]
        return moved(x, px), moved(y, py)

    def beside(half, first, second):
        return device(*at(half, first, second), z, core)

    other = device(x, y, z, 1 - core)
    x_rows = [moved(x, d) * 1024 for d in range(4)]
    y_rows = [lax.div(moved(y, d), 2) * 512 + lax.rem(moved(y, d), 2) * 16 for d in range(4)]
    z_rows = [moved(z, d, 8) * 32 + core * 256 for d in range(8)]

    def chunk(unit, first, second):
        d, half = UNITS[unit]
        px, py = ((first, second), (second, first))[half]
        return ordered.at[pl.ds(pl.multiple_of(x_rows[px % 4] + y_rows[py % 4] + z_rows[d], 16), 16)]

    def send(ref, send_sem, recv_sem, to):
        pltpu.make_async_remote_copy(
            src_ref=ref, dst_ref=ref, send_sem=send_sem, recv_sem=recv_sem, device_id=to, device_id_type=MESH
        ).start()

    def wait(chunks, sem):
        ref = ordered.at[pl.ds(0, 16 * chunks)]
        pltpu.make_async_copy(ref, ref, sem).wait()

    barrier = pltpu.get_barrier_semaphore()
    peers = [device(x, y, moved(z, d, 8), core) for d in range(1, 8)]
    peers += [beside(half, d, 0) for half in range(2) for d in range(1, 4)] + [other]
    for peer in peers:
        pl.semaphore_signal(barrier, inc=1, device_id=peer, device_id_type=MESH)
    local_copy = pltpu.make_async_copy(own, chunk(0, 0, 0), copied)
    local_copy.start()
    ordered[2 * ROWS :, :] = jnp.zeros((8, LANES), jnp.float32)
    pl.semaphore_wait(barrier, len(peers))

    def to_second(unit, j):
        half = UNITS[unit][1]
        for e in (1, 3, 2):
            send(
                chunk(unit, j, 0), second_send.at[unit], second_recv.at[unit * 3 + e - 1], beside(half, 0, e)
            )

    def to_core(unit, e):
        for j in range(4):
            send(chunk(unit, j, e), core_send.at[unit], core_recv.at[unit], other)

    def begin(unit):
        half = UNITS[unit][1]
        for e in (1, 3, 2):
            send(chunk(unit, 0, 0), first_send.at[unit], first_recv.at[unit], beside(half, e, 0))
        to_second(unit, 0)

    def z_done(unit):
        wait(1, z_recv.at[unit - 1])
        begin(unit)

    def first_done(unit):
        wait(3, first_recv.at[unit])
        for j in (1, 3, 2):
            to_second(unit, j)
        to_core(unit, 0)

    def second_done(unit):
        for e in (1, 3, 2):
            wait(4, second_recv.at[unit * 3 + e - 1])
            to_core(unit, -e)

    mine = x_rows[0] + y_rows[0] + z_rows[0]
    local_copy.wait()
    for unit in range(1, 8):
        d = UNITS[unit][0]
        ref = ordered.at[pl.ds(pl.multiple_of(mine, 16), 16)]
        send(ref, z_send.at[unit - 1], z_recv.at[unit - 1], device(x, y, moved(z, -d, 8), core))
    begin(0)
    first_weights(weights)
    z_done(1)
    z_done(2)
    first_done(0)
    for unit in range(3, 8):
        z_done(unit)
    second_tables(second)
    first_done(1)
    first_done(2)
    second_done(0)
    for unit in range(3, 8):
        first_done(unit)
    for unit in range(1, 8):
        second_done(unit)
    for unit in range(8):
        wait(16, core_recv.at[unit])
    channelize(ordered, weights, base)
    for unit in range(8):
        if unit:
            wait(1, z_send.at[unit - 1])
        wait(3, first_send.at[unit])
        wait(12, second_send.at[unit])
        wait(16, core_send.at[unit])


def gather(tiles):
    def sems(count):
        return pltpu.SemaphoreType.DMA((count,))

    far = pl.BlockSpec(memory_space=pltpu.HBM)
    near = pl.BlockSpec(memory_space=pltpu.VMEM)
    return pl.pallas_call(
        gather_kernel,
        out_shape=[
            jax.ShapeDtypeStruct((LANES * WINDOWS, LANES), jnp.float32),
            jax.ShapeDtypeStruct((2, 2, 256, 256), jnp.bfloat16),
        ],
        in_specs=[far],
        out_specs=[near] * 2,
        scratch_shapes=[
            pltpu.VMEM((2 * ROWS + 8, LANES), jnp.float32),
            pltpu.VMEM((DEPTH, 2 * LANES), jnp.bfloat16),
            pltpu.SemaphoreType.DMA,
            sems(7), sems(7), sems(8), sems(8), sems(8), sems(24), sems(8), sems(8),
        ],
        compiler_params=pltpu.CompilerParams(
            collective_id=0, has_side_effects=True, vmem_limit_bytes=VMEM_LIMIT
        ),
    )(tiles)


def local(record):
    tiles = record.reshape(2, 8, LANES).transpose(1, 0, 2).reshape(16, LANES)
    tiles = pltpu.with_memory_space_constraint(tiles, pltpu.HBM)
    result = spectra(*gather(tiles))
    result = result.reshape(WIDTH, WIDTH, WINDOWS, 2, 2, LANES)
    result = result.transpose(0, 1, 2, 4, 3, 5)
    return result.reshape(WIDTH, WIDTH, WINDOWS, 2, 2 * LANES)


def solution(mesh):
    return jax.shard_map(
        local,
        mesh=mesh,
        in_specs=(P(None, ("row", "col")),),
        out_specs=P("row", "col", None, None, None),
        check_vma=False,
    )
```

```python
import math

import jax
import jax.numpy as jnp
import numpy as np
from jax import lax
from jax.experimental import pallas as pl
from jax.experimental.pallas import tpu as pltpu
from jax.sharding import PartitionSpec as P

C = 256
P_SIZE = 256
HOP = 64
LANES = 128
WIDTH = 16
WINDOWS = 16
ROWS = 2048
PIECES = 3
DEPTH = PIECES * 2 * LANES
MESH = pl.DeviceIdType.MESH
UNITS = ((0, 0), (1, 1), (7, 0), (2, 1), (6, 0), (3, 1), (5, 0), (4, 1))
SLOTS = 4
GROUP = 4
VMEM_LIMIT = 16 * 2**20


def cosine_series():
    nodes = 0.5 - 0.5 * np.cos(np.pi * (np.arange(64) + 0.5) / 64)
    fit = np.polynomial.chebyshev.Chebyshev.fit(nodes, -np.cos(np.pi * np.sqrt(nodes)), 8, domain=[0, 1])
    return [float(c) for c in fit.convert(kind=np.polynomial.Polynomial).coef]


SERIES = cosine_series()


def cosine(turns):
    w = ((turns & 255) - 128).astype(jnp.float32) * (1.0 / 128)
    square = w * w
    result = jnp.full(w.shape, SERIES[-1], jnp.float32)
    for c in SERIES[-2::-1]:
        result = result * square + c
    return result


def grid_of(dim):
    return lax.broadcasted_iota(jnp.int32, (LANES, LANES), dim)


def halves(value):
    high = value.astype(jnp.bfloat16)
    low = (value - high.astype(jnp.float32)).astype(jnp.bfloat16)
    return high, low


def dot(a, b):
    return lax.dot_general(a, b, (((1,), (0,)), ((), ())), preferred_element_type=jnp.float32)


def first_weights(weights):
    column = grid_of(1)
    block = jnp.where(column < 64, lax.axis_index("row"), lax.axis_index("col"))
    channel = block * WIDTH + column % WIDTH
    odd = (column // 32) % 2
    imag = (column // 16) % 2
    for piece in range(PIECES):
        position = grid_of(0) + piece * LANES
        m = position - HOP * odd
        window = (0.5 - 0.5 * cosine(m)) * (1.0 / math.sqrt(3 * C / 8))
        window = jnp.where((m >= 0) & (m < C), window, 0.0)
        for part in range(2):
            shift = 64 * imag if part == 0 else 192 * (1 - imag)
            high, low = halves(window * cosine(channel * position + shift))
            start = (2 * piece + part) * LANES
            weights[start : start + LANES, :LANES] = high
            weights[start : start + LANES, LANES:] = low


def second_tables(second):
    for parity in range(2):
        turns = (2 * grid_of(0) + parity) * grid_of(1)
        plain = cosine(turns) * (1.0 / 16)
        for part in range(2):
            for imag in range(2):
                value = plain if part == imag else cosine(turns + (64 if imag else 192)) * (1.0 / 16)
                high, low = halves(value)
                rows = slice(part * LANES, (part + 1) * LANES)
                columns = slice(imag * LANES, (imag + 1) * LANES)
                second[0, parity, rows, columns] = high
                second[1, parity, rows, columns] = low


def channelize(ordered, weights, base):
    step = 1024
    sign = (1 - 2 * (grid_of(0) & grid_of(1) & 1)).astype(jnp.float32)

    def block(i, _):
        start = pl.multiple_of(i * (2 * step), 2 * step)
        pieces = [ordered[pl.ds(start + j, step, stride=2), :] for j in range(2 * PIECES)]
        high, low = halves(jnp.concatenate(pieces, axis=1))
        wide = dot(jnp.concatenate([high, low], axis=0), weights[...])
        result = wide[:step, :LANES] + wide[:step, LANES:] + wide[step:, :LANES]
        for k in range(step // LANES):
            turned = result[k * LANES : (k + 1) * LANES].T * sign
            base[pl.ds(i * (step // LANES) + k, LANES, stride=WINDOWS), :] = turned
        return 0

    lax.fori_loop(0, ROWS // step, block, 0, unroll=True)


def correlate(step, base, second, out):
    count = GROUP * 256

    def tile(first, channels):
        return base[pl.ds(pl.multiple_of(first * WINDOWS, WINDOWS), channels * WINDOWS), :]

    sums = []
    for parity in range(2):
        lead_re = tile(parity * 32 + step * GROUP, GROUP).reshape(GROUP, 1, WINDOWS, LANES)
        lead_im = tile(parity * 32 + 16 + step * GROUP, GROUP).reshape(GROUP, 1, WINDOWS, LANES)
        trail_re = tile(64 + parity * 32, 16).reshape(1, WIDTH, WINDOWS, LANES)
        trail_im = tile(64 + parity * 32 + 16, 16).reshape(1, WIDTH, WINDOWS, LANES)
        real = (lead_re * trail_re + lead_im * trail_im).reshape(count, LANES)
        imag = (lead_im * trail_re - lead_re * trail_im).reshape(count, LANES)
        high, low = halves(jnp.concatenate([real, imag], axis=1))
        both = dot(jnp.concatenate([high, low], axis=0), second[0, parity])
        sums.append(both[:count] + both[count:] + dot(high, second[1, parity]))
    total = sums[0] + sums[1]
    rest = sums[0] - sums[1]
    for j, value in enumerate((total[:, :LANES], total[:, LANES:], rest[:, :LANES], rest[:, LANES:])):
        out[pl.ds(j, count, stride=4), :] = value


def kernel(base, second, out, buffer, sems):
    size = GROUP * 1024
    steps = WIDTH // GROUP

    def store(a, slot):
        place = pl.ds(pl.multiple_of(a * size, size), size)
        return pltpu.make_async_copy(buffer.at[slot], out.at[place], sems.at[slot])

    def step(a, _):
        slot = lax.rem(a, SLOTS)

        @pl.when(a >= SLOTS)
        def _():
            store(a, slot).wait()

        correlate(a, base, second, buffer.at[slot])
        store(a, slot).start()
        return 0

    lax.fori_loop(0, steps, step, 0, unroll=True)
    for a in range(steps - SLOTS, steps):
        store(a, a % SLOTS).wait()


def spectra(base, second):
    whole = pl.BlockSpec(memory_space=pltpu.VMEM)
    return pl.pallas_call(
        kernel,
        out_shape=jax.ShapeDtypeStruct((WIDTH * 1024, LANES), jnp.float32),
        in_specs=[whole, whole],
        out_specs=pl.BlockSpec(memory_space=pl.ANY),
        scratch_shapes=[pltpu.VMEM((SLOTS, GROUP * 1024, LANES), jnp.float32), pltpu.SemaphoreType.DMA((SLOTS,))],
        compiler_params=pltpu.CompilerParams(vmem_limit_bytes=VMEM_LIMIT),
    )(base, second)


def gather_kernel(
    own, base, second, ordered, weights, copied,
    z_send, z_recv, first_send, first_recv, second_send, second_recv, core_send, core_recv
):
    row = lax.axis_index("row")
    col = lax.axis_index("col")
    core = lax.rem(row, 2)
    x = lax.div(row, 4)
    y = lax.rem(lax.div(row, 2), 2) * 2 + lax.rem(col, 2)
    z = lax.div(col, 2)

    def moved(value, distance, length=4):
        return lax.rem(value + (distance + length), length) if distance else value

    def device(x, y, z, core):
        return (x * 4 + lax.div(y, 2) * 2 + core, z * 2 + lax.rem(y, 2))

    def at(half, first, second):
        px, py = ((first, second), (second, first))[half]
        return moved(x, px), moved(y, py)

    def beside(half, first, second):
        return device(*at(half, first, second), z, core)

    other = device(x, y, z, 1 - core)
    x_rows = [moved(x, d) * 1024 for d in range(4)]
    y_rows = [lax.div(moved(y, d), 2) * 512 + lax.rem(moved(y, d), 2) * 16 for d in range(4)]
    z_rows = [moved(z, d, 8) * 32 + core * 256 for d in range(8)]

    def chunk(unit, first, second):
        d, half = UNITS[unit]
        px, py = ((first, second), (second, first))[half]
        return ordered.at[pl.ds(pl.multiple_of(x_rows[px % 4] + y_rows[py % 4] + z_rows[d], 16), 16)]

    def send(ref, send_sem, recv_sem, to):
        pltpu.make_async_remote_copy(
            src_ref=ref, dst_ref=ref, send_sem=send_sem, recv_sem=recv_sem, device_id=to, device_id_type=MESH
        ).start()

    def wait(chunks, sem):
        ref = ordered.at[pl.ds(0, 16 * chunks)]
        pltpu.make_async_copy(ref, ref, sem).wait()

    barrier = pltpu.get_barrier_semaphore()
    peers = [device(x, y, moved(z, d, 8), core) for d in range(1, 8)]
    peers += [beside(half, d, 0) for half in range(2) for d in range(1, 4)] + [other]
    for peer in peers:
        pl.semaphore_signal(barrier, inc=1, device_id=peer, device_id_type=MESH)
    local_copy = pltpu.make_async_copy(own, chunk(0, 0, 0), copied)
    local_copy.start()
    ordered[2 * ROWS :, :] = jnp.zeros((8, LANES), jnp.float32)
    pl.semaphore_wait(barrier, len(peers))

    def to_second(unit, j):
        half = UNITS[unit][1]
        for e in (1, 3, 2):
            send(
                chunk(unit, j, 0), second_send.at[unit], second_recv.at[unit * 3 + e - 1], beside(half, 0, e)
            )

    def to_core(unit, e):
        for j in range(4):
            send(chunk(unit, j, e), core_send.at[unit], core_recv.at[unit], other)

    def begin(unit):
        half = UNITS[unit][1]
        for e in (1, 3, 2):
            send(chunk(unit, 0, 0), first_send.at[unit], first_recv.at[unit], beside(half, e, 0))
        to_second(unit, 0)

    def z_done(unit):
        wait(1, z_recv.at[unit - 1])
        begin(unit)

    def first_done(unit):
        wait(3, first_recv.at[unit])
        for j in (1, 3, 2):
            to_second(unit, j)
        to_core(unit, 0)

    def second_done(unit):
        for e in (1, 3, 2):
            wait(4, second_recv.at[unit * 3 + e - 1])
            to_core(unit, -e)

    mine = x_rows[0] + y_rows[0] + z_rows[0]
    local_copy.wait()
    for unit in range(1, 8):
        d = UNITS[unit][0]
        ref = ordered.at[pl.ds(pl.multiple_of(mine, 16), 16)]
        send(ref, z_send.at[unit - 1], z_recv.at[unit - 1], device(x, y, moved(z, -d, 8), core))
    begin(0)
    first_weights(weights)
    z_done(1)
    z_done(2)
    first_done(0)
    for unit in range(3, 8):
        z_done(unit)
    second_tables(second)
    first_done(1)
    first_done(2)
    second_done(0)
    for unit in range(3, 8):
        first_done(unit)
    for unit in range(1, 8):
        second_done(unit)
    for unit in range(8):
        wait(16, core_recv.at[unit])
    channelize(ordered, weights, base)
    for unit in range(8):
        if unit:
            wait(1, z_send.at[unit - 1])
        wait(3, first_send.at[unit])
        wait(12, second_send.at[unit])
        wait(16, core_send.at[unit])


def gather(tiles):
    def sems(count):
        return pltpu.SemaphoreType.DMA((count,))

    far = pl.BlockSpec(memory_space=pltpu.HBM)
    near = pl.BlockSpec(memory_space=pltpu.VMEM)
    return pl.pallas_call(
        gather_kernel,
        out_shape=[
            jax.ShapeDtypeStruct((LANES * WINDOWS, LANES), jnp.float32),
            jax.ShapeDtypeStruct((2, 2, 256, 256), jnp.bfloat16),
        ],
        in_specs=[far],
        out_specs=[near] * 2,
        scratch_shapes=[
            pltpu.VMEM((2 * ROWS + 8, LANES), jnp.float32),
            pltpu.VMEM((DEPTH, 2 * LANES), jnp.bfloat16),
            pltpu.SemaphoreType.DMA,
            sems(7), sems(7), sems(8), sems(8), sems(8), sems(24), sems(8), sems(8),
        ],
        compiler_params=pltpu.CompilerParams(
            collective_id=0, has_side_effects=True, vmem_limit_bytes=VMEM_LIMIT
        ),
    )(tiles)


def local(record):
    tiles = record.reshape(2, 8, LANES).transpose(1, 0, 2).reshape(16, LANES)
    tiles = pltpu.with_memory_space_constraint(tiles, pltpu.HBM)
    result = spectra(*gather(tiles))
    result = result.reshape(WIDTH, WIDTH, WINDOWS, 2, 2, LANES)
    result = result.transpose(0, 1, 2, 4, 3, 5)
    return result.reshape(WIDTH, WIDTH, WINDOWS, 2, 2 * LANES)


def solution(mesh):
    return jax.shard_map(
        local,
        mesh=mesh,
        in_specs=(P(None, ("row", "col")),),
        out_specs=P("row", "col", None, None, None),
        check_vma=False,
    )
```
